32 devices in a mesh: member: 8 (over z, core), basin: 4 (over y, x).
Axes of the slice: x: 2, y: 2, z: 4, core: 2. Of those that a mesh axis runs over, the one named last changes fastest.
Arguments:
- prior_params: float32 [256, 8, 512], P('member', None, 'basin'), may hold values from -3 to 3
- lateral_flow: float32 [256, 2, 65536], P('member', None, 'basin'), may hold values from 0.2 to 2
- inflow_start: float32 [65536], P('basin'), may hold values from 0.5 to 4
- outflow_start: float32 [65536], P('basin'), may hold values from 0.5 to 4
- reach_count: int32 [512], P('basin'), may hold values from 64 to 128
- downstream: int32 [512], P('basin'), may hold values from 0 to 63
- gauge_reach: int32 [2048], P('basin'), may hold values from 0 to 16383
- observed: float32 [2, 2048], P(None, 'basin'), may hold values from 0.5 to 4
- obs_var: float32 [2, 2048], P(None, 'basin'), may hold values from 0.02 to 0.5
- obs_noise: float32 [256, 2, 2048], P('member', None, 'basin'), may hold values from -4 to 4
Outputs:
- posterior: float32 [256, 8, 512], P('member', None, 'basin')
- predicted: float32 [256, 2, 2048], P('member', None, 'basin')
The draws below stay inside these ranges and needn't reach their ends.
All inputs are finite; a program needn't handle non-finite values.
Results may differ from the reference program's by a relative error of at most 0.0003.
Values sent between devices are 32-bit elements; how exact they have to be, the bound alone decides.
A program may use at most 128 MiB of HBM per device.

```python
import math
import jax
import jax.numpy as jnp
from jax import lax

LANES = 128
NPAR = 8
HOURS = 2
M_DEV = 32
BLK_LEV = 64
LEV_DEV = 2
GAUGE_DEV = 512
MEMBERS = 256
LEVELS = 8
BLOCKS = 512
REACHES = 65536
GAUGES = 2048
N_MEMBER = 8


def draw_reach_count(key, part):
    counts = jax.random.randint(key, (BLOCKS,), 64, 129, dtype=jnp.int32)
    return counts.at[0].set(128)


def with_ends(array, key, low, high):
    spot = [jax.random.randint(jax.random.fold_in(key, axis), (), 0, length) for axis, length in enumerate(array.shape)]
    longest = array.shape.index(max(array.shape))
    neighbour = spot[:longest] + [(spot[longest] + 1) % array.shape[longest]] + spot[longest + 1:]
    return array.at[tuple(spot)].set(low).at[tuple(neighbour)].set(high)


def level_of(stream_key, shape, split, least, top_value):
    loudness = 1.0
    for dim, shards_of in split:
        draws = jax.random.uniform(jax.random.fold_in(jax.random.fold_in(stream_key, 6), dim), (shards_of,), jnp.float32, least / len(split), top_value / len(split))
        loudness = loudness * jnp.repeat(jnp.exp(draws), shape[dim] // shards_of).reshape((-1,) + (1,) * (len(shape) - 1 - dim))
    return loudness


def scatter_about(key, shape, deviation, most, shards=(), kind=jnp.bfloat16):
    loudness = level_of(key, shape, shards, -0.22, 0.18) if shards else 1.0
    entries = jax.random.normal(key, shape, jnp.float32) * deviation * loudness
    return jnp.minimum(jnp.maximum(entries, -most), most).astype(kind)


def setup_inputs(seed: int = 0) -> dict:
    seeds = jax.random.split(jax.random.key(seed), 11)
    prior_params = scatter_about(seeds[0], (MEMBERS, NPAR, BLOCKS), 0.7, 3.0, ((0, 8), (2, 4)), jnp.float32)
    lateral_flow = jnp.clip(jnp.exp(math.log(2.0) - 2.3025851 * jax.random.uniform(seeds[1], (MEMBERS, HOURS, REACHES), jnp.float32) ** level_of(seeds[1], (MEMBERS, HOURS, REACHES), ((0, 8), (2, 4)), -0.2, 0.2)), 0.2, 2.0)
    inflow_start = jnp.clip(0.5 + 3.5 * jax.random.uniform(seeds[2], (REACHES,), jnp.float32) ** level_of(seeds[2], (REACHES,), ((0, 4),), -0.2, 0.2), 0.5, 4.0)
    outflow_start = jnp.clip(0.5 + 3.5 * jax.random.uniform(seeds[3], (REACHES,), jnp.float32) ** level_of(seeds[3], (REACHES,), ((0, 4),), -0.2, 0.2), 0.5, 4.0)
    reach_count = draw_reach_count(jax.random.fold_in(seeds[10], 71), 0)
    downstream = with_ends(jax.random.randint(seeds[5], (BLOCKS,), 0, BLK_LEV), jax.random.fold_in(seeds[5], 1), 0, BLK_LEV - 1).astype(jnp.int32)
    gauge_reach = with_ends(jax.random.randint(seeds[6], (GAUGES,), 0, BLK_LEV * LEV_DEV * LANES), jax.random.fold_in(seeds[6], 1), 0, (BLK_LEV * LEV_DEV * LANES) - 1).astype(jnp.int32)
    observed = jnp.clip(0.5 + 3.5 * jax.random.uniform(seeds[7], (HOURS, GAUGES), jnp.float32) ** level_of(seeds[7], (HOURS, GAUGES), ((1, 4),), -0.2, 0.2), 0.5, 4.0)
    obs_var = jnp.clip(jnp.exp(math.log(0.5) - 3.218876 * jax.random.uniform(seeds[8], (HOURS, GAUGES), jnp.float32) ** level_of(seeds[8], (HOURS, GAUGES), ((1, 4),), -0.2, 0.2)), 0.02, 0.5)
    obs_noise = scatter_about(seeds[9], (MEMBERS, HOURS, GAUGES), 1.0, 4.0, ((0, 8), (2, 4)), jnp.float32)
    return dict(prior_params=prior_params, lateral_flow=lateral_flow, inflow_start=inflow_start, outflow_start=outflow_start, reach_count=reach_count, downstream=downstream, gauge_reach=gauge_reach, observed=observed, obs_var=obs_var, obs_noise=obs_noise)


exact_mode = lax.Precision.HIGHEST

def inverse_sinh(values):
    return jnp.log(values + jnp.sqrt(values * values + 1.0))

def route_coefficients(prior_params):
    storage = 0.02 + 0.1 * jax.nn.sigmoid(prior_params[:, 0, :])
    weighting = 0.2 * jax.nn.sigmoid(prior_params[:, 1, :])
    denominator = storage * (1.0 - weighting) + 0.5
    weight_now = (0.5 - storage * weighting) / denominator
    weight_back = (0.5 + storage * weighting) / denominator
    weight_carry = (storage * (1.0 - weighting) - 0.5) / denominator
    return (weight_now[:, :, None], weight_back[:, :, None], weight_carry[:, :, None])

def lateral_scaling(prior_params, lane_count):
    lane_pos = jnp.arange(lane_count, dtype=jnp.float32)
    orders = jnp.arange(6, dtype=jnp.float32)
    cosine_modes = jnp.cos(math.pi * orders[:, None] * (lane_pos[None, :] + 0.5) / lane_count)
    exponent = jnp.einsum('mkb,kr->mbr', 0.2 * prior_params[:, 2:, :], cosine_modes, precision=exact_mode)
    return jnp.exp(exponent)

def solve_gram(gram_matrix, cross_matrix):
    factor = jnp.linalg.cholesky(gram_matrix)
    halfway = lax.linalg.triangular_solve(factor, cross_matrix, left_side=True, lower=True)
    return lax.linalg.triangular_solve(factor, halfway, left_side=True, lower=True, transpose_a=True)

def to_levels(values, group_size):
    shaped = values.reshape((group_size, LEVELS, BLK_LEV) + values.shape[2:])
    return jnp.moveaxis(shaped, 1, 0)

def reference(prior_params, lateral_flow, inflow_start, outflow_start, reach_count, downstream, gauge_reach, observed, obs_var, obs_noise):
    lane_ids = jnp.arange(LANES, dtype=jnp.int32)
    live_mask = (lane_ids[None, :] < reach_count[:, None]).astype(jnp.float32).reshape(LEVELS, BLK_LEV, LANES)
    targets = jnp.arange(BLK_LEV, dtype=jnp.int32)
    one_hot = (downstream.reshape(LEVELS, BLK_LEV)[:, None, :] == targets[None, :, None]).astype(jnp.float32)
    start_in = inflow_start.reshape(LEVELS, BLK_LEV, LANES) * live_mask
    start_out = outflow_start.reshape(LEVELS, BLK_LEV, LANES) * live_mask
    flat_index = jnp.arange(GAUGES, dtype=jnp.int32) // GAUGE_DEV * (BLK_LEV * LEV_DEV * LANES) + gauge_reach

    def one_group(operands):
        prior_group, lateral_group = operands
        group_size = prior_group.shape[0]
        weight_now, weight_back, weight_carry = route_coefficients(prior_group)
        scaling = lateral_scaling(prior_group, LANES)
        now_lev = to_levels(weight_now, group_size)
        back_lev = to_levels(weight_back, group_size)
        carry_lev = to_levels(weight_carry, group_size)
        scale_lev = to_levels(scaling, group_size)
        prev_in = jnp.broadcast_to(start_in[:, None], (LEVELS, group_size, BLK_LEV, LANES))
        prev_out = jnp.broadcast_to(start_out[:, None], (LEVELS, group_size, BLK_LEV, LANES))
        results = []
        for hour_idx in range(HOURS):
            lateral_lev = to_levels(lateral_group[:, hour_idx].reshape(group_size, BLOCKS, LANES), group_size)

            def level_step(upstream, pieces):
                coef_now, coef_back, coef_carry, scale_now, lateral_now, mask_now, hot_now, old_in, old_out = pieces
                inflow = mask_now * (lateral_now * scale_now + upstream)
                outflow = coef_now * inflow + coef_back * old_in + coef_carry * old_out
                downstream_in = jnp.einsum('nj,gjr->gnr', hot_now, outflow, precision=exact_mode)
                return (downstream_in, (inflow, outflow))
            initial = jnp.zeros((group_size, BLK_LEV, LANES), jnp.float32)
            _, (prev_in, prev_out) = lax.scan(level_step, initial, (now_lev, back_lev, carry_lev, scale_lev, lateral_lev, live_mask, one_hot, prev_in, prev_out))
            flat = jnp.moveaxis(prev_out, 0, 1).reshape(group_size, REACHES)
            results.append(inverse_sinh(flat[:, flat_index]))
        return jnp.stack(results, 1)
    grouped = lax.map(one_group, (prior_params.reshape(N_MEMBER, M_DEV, NPAR, BLOCKS), lateral_flow.reshape(N_MEMBER, M_DEV, HOURS, REACHES)))
    predicted = grouped.reshape(MEMBERS, HOURS, GAUGES)
    spread = jnp.sqrt(obs_var)
    spread_root = math.sqrt(MEMBERS - 1.0)
    mean_pred = lax.optimization_barrier(jnp.sum(predicted, 0)) / MEMBERS
    scaled = (predicted - mean_pred) / (spread_root * (2.0 * spread))
    innovation = (observed + 2.0 * spread * obs_noise - predicted) / (2.0 * spread)
    scaled_rows = scaled.reshape(MEMBERS, HOURS * GAUGES)
    innov_rows = innovation.reshape(MEMBERS, HOURS * GAUGES)
    gram_matrix = jnp.dot(scaled_rows.astype(jnp.float32), scaled_rows.T.astype(jnp.float32), precision=exact_mode, preferred_element_type=jnp.float32)
    cross_matrix = jnp.dot(scaled_rows.astype(jnp.float32), innov_rows.T.astype(jnp.float32), precision=exact_mode, preferred_element_type=jnp.float32)
    gram_matrix = gram_matrix + jnp.eye(MEMBERS, dtype=jnp.float32)
    solved = solve_gram(gram_matrix, cross_matrix)
    mean_prior = lax.optimization_barrier(jnp.sum(prior_params, 0)) / MEMBERS
    anomaly = (prior_params - mean_prior) / spread_root
    posterior = prior_params + jnp.einsum('mn,mkb->nkb', solved, anomaly, precision=exact_mode)
    return (posterior, predicted)
```

```python
import functools
import math

import jax
import jax.numpy as jnp
from jax import lax
import numpy as np
from jax.experimental import pallas as pl
from jax.experimental.pallas import tpu as pltpu
from jax.sharding import PartitionSpec as P

LANES = 128
BLK_LEV = 64
exact_mode = lax.Precision.HIGHEST
VMEM = pltpu.VMEM
SMEM = pltpu.SMEM
MESH = pl.DeviceIdType.MESH


def vmem_spec():
    return pl.BlockSpec(memory_space=VMEM)


def smem_spec():
    return pl.BlockSpec(memory_space=SMEM)


def exchange_body(axis, n, spread_out, x_ref, o_ref, send_sem, recv_sem, own_sem):
    me = lax.axis_index(axis)
    barrier = pltpu.get_barrier_semaphore()
    for i in range(1, n):
        pl.semaphore_signal(
            barrier, inc=1, device_id={axis: lax.rem(me + i, n)}, device_id_type=MESH
        )
    pl.semaphore_wait(barrier, n - 1)
    copies = []
    for i in range(1, n):
        peer = lax.rem(me + i, n)
        copies.append(
            pltpu.make_async_remote_copy(
                src_ref=x_ref.at[peer] if spread_out else x_ref,
                dst_ref=o_ref.at[me],
                send_sem=send_sem.at[i - 1],
                recv_sem=recv_sem.at[i - 1],
                device_id={axis: peer},
                device_id_type=MESH,
            )
        )
    for copy in copies:
        copy.start()
    own = pltpu.make_async_copy(x_ref.at[me] if spread_out else x_ref, o_ref.at[me], own_sem)
    own.start()
    own.wait()
    for copy in copies:
        copy.wait()


def exchange(x, axis, collective_id, spread_out=False):
    n = lax.axis_size(axis)
    shape = x.shape if spread_out else (n,) + x.shape
    return pl.pallas_call(
        functools.partial(exchange_body, axis, n, spread_out),
        out_shape=jax.ShapeDtypeStruct(shape, x.dtype),
        in_specs=[vmem_spec()],
        out_specs=vmem_spec(),
        scratch_shapes=[
            pltpu.SemaphoreType.DMA((n - 1,)),
            pltpu.SemaphoreType.DMA((n - 1,)),
            pltpu.SemaphoreType.DMA,
        ],
        compiler_params=pltpu.CompilerParams(collective_id=collective_id, has_side_effects=True),
        name=f"exchange_{collective_id}",
    )(x)


def doubling_bits(n):
    bits = []
    bit = n // 2
    while bit:
        bits.append(bit)
        bit //= 2
    return bits


def observed_body(
    hours, n_basin, n, x_ref, o_ref, land_ref, part_send, part_recv, send_sem, recv_sem
):
    basin = lax.axis_index("basin")
    me = lax.axis_index("member")
    partners = [me + bit * (1 - 2 * lax.rem(me // bit, 2)) for bit in doubling_bits(n)]
    barrier = pltpu.get_barrier_semaphore()
    for i in range(1, n_basin):
        pl.semaphore_signal(
            barrier, inc=1, device_id={"basin": lax.rem(basin + i, n_basin)}, device_id_type=MESH
        )
    for partner in partners:
        pl.semaphore_signal(barrier, inc=1, device_id={"member": partner}, device_id_type=MESH)
    pl.semaphore_wait(barrier, n_basin - 1 + len(partners))
    parts = []
    for i in range(1, n_basin):
        peer = lax.rem(basin + i, n_basin)
        parts.append(
            pltpu.make_async_remote_copy(
                src_ref=x_ref.at[peer], dst_ref=land_ref.at[i - 1],
                send_sem=part_send.at[i - 1], recv_sem=part_recv.at[i - 1],
                device_id={"basin": peer}, device_id_type=MESH,
            )
        )
    for copy in parts:
        copy.start()
    for copy in parts:
        copy.wait()
    flows = x_ref[basin]
    for i in range(1, n_basin):
        flows = flows + land_ref[i - 1]
    pred = inverse_sinh(flows)
    rows = o_ref.shape[1]
    gauges = x_ref.shape[2]
    for h in range(hours):
        o_ref[0, :, h * gauges : (h + 1) * gauges] = pred[h * rows : (h + 1) * rows]

    copies = {}
    for p in range(n):
        if p:
            copies[p].wait_recv()
        for k, partner in enumerate(partners):
            to = 2**k + p
            if p < 2**k:
                copies[to] = pltpu.make_async_remote_copy(
                    src_ref=o_ref.at[p], dst_ref=o_ref.at[to],
                    send_sem=send_sem.at[to - 1], recv_sem=recv_sem.at[to - 1],
                    device_id={"member": partner}, device_id_type=MESH,
                )
                copies[to].start()
    for p in range(1, n):
        copies[p].wait_send()


def observed_gather(parts, hours, collective_id):
    n = lax.axis_size("member")
    n_basin = lax.axis_size("basin")
    rows, gauges = parts.shape[1] // hours, parts.shape[2]
    return pl.pallas_call(
        functools.partial(observed_body, hours, n_basin, n),
        out_shape=jax.ShapeDtypeStruct((n, rows, hours * gauges), parts.dtype),
        in_specs=[vmem_spec()],
        out_specs=vmem_spec(),
        scratch_shapes=[
            VMEM((n_basin - 1,) + parts.shape[1:], parts.dtype),
            pltpu.SemaphoreType.DMA((n_basin - 1,)),
            pltpu.SemaphoreType.DMA((n_basin - 1,)),
            pltpu.SemaphoreType.DMA((n - 1,)),
            pltpu.SemaphoreType.DMA((n - 1,)),
        ],
        compiler_params=pltpu.CompilerParams(collective_id=collective_id, has_side_effects=True),
        name=f"observed_{collective_id}",
    )(parts)


def sum_body(axis, n, x_ref, o_ref, land_ref, sem1, sem2, sem3, sem4):
    me = lax.axis_index(axis)
    barrier = pltpu.get_barrier_semaphore()
    for i in range(1, n):
        pl.semaphore_signal(
            barrier, inc=1, device_id={axis: lax.rem(me + i, n)}, device_id_type=MESH
        )
    pl.semaphore_wait(barrier, n - 1)
    copies = []
    for i in range(1, n):
        peer = lax.rem(me + i, n)
        copies.append(
            pltpu.make_async_remote_copy(
                src_ref=x_ref.at[peer], dst_ref=land_ref.at[i - 1],
                send_sem=sem1.at[i - 1], recv_sem=sem2.at[i - 1],
                device_id={axis: peer}, device_id_type=MESH,
            )
        )
    for copy in copies:
        copy.start()
    for copy in copies:
        copy.wait()
    total = x_ref[me]
    for i in range(1, n):
        total = total + land_ref[i - 1]
    o_ref[me] = total
    copies = []
    for i in range(1, n):
        copies.append(
            pltpu.make_async_remote_copy(
                src_ref=o_ref.at[me], dst_ref=o_ref.at[me],
                send_sem=sem3.at[i - 1], recv_sem=sem4.at[i - 1],
                device_id={axis: lax.rem(me + i, n)}, device_id_type=MESH,
            )
        )
    for copy in copies:
        copy.start()
    for copy in copies:
        copy.wait()


def sum_over(x, axis, collective_id):
    n = lax.axis_size(axis)
    return pl.pallas_call(
        functools.partial(sum_body, axis, n),
        out_shape=jax.ShapeDtypeStruct(x.shape, x.dtype),
        in_specs=[vmem_spec()],
        out_specs=vmem_spec(),
        scratch_shapes=[VMEM((n - 1,) + x.shape[1:], x.dtype)]
        + [pltpu.SemaphoreType.DMA((n - 1,))] * 4,
        compiler_params=pltpu.CompilerParams(collective_id=collective_id, has_side_effects=True),
        name=f"sum_{collective_id}",
    )(x)


def permuted_step(held, axis, bit):
    n = lax.axis_size(axis)
    other = lax.ppermute(held, axis, [(i, i ^ bit) for i in range(n)])
    return jnp.concatenate([held, other], 0)


def split_two(values):
    high = values.astype(jnp.bfloat16)
    low = (values - high.astype(jnp.float32)).astype(jnp.bfloat16)
    return jnp.concatenate([high, low], axis=1)


def route_body(
    seg_count, level_count, members, gauges, hours, param_count,
    basin_ref, meta_ref, prior_ref, cos_ref, pin_ref, pout_ref, lat_hbm,
    out_ref,
    up_ref, flow_ref, row_ref, now_ref, back_ref, carry_ref, par_ref, raw_ref, ready_ref,
    int_ref, table_ref, sem, table_sem,
):
    first = basin_ref[0]
    lev = BLK_LEV
    seg_blocks = level_count * lev
    rows = members
    packs = LANES // members
    shape = (rows, LANES)
    lane = lax.broadcasted_iota(jnp.int32, shape, 1)
    place = (lane // members) * members + lax.broadcasted_iota(jnp.int32, shape, 0)

    chunks = sem.shape[0]
    chunk_rows = seg_blocks * hours // chunks

    def fetch(c, m):
        span = pl.ds(c * chunk_rows, chunk_rows)
        return pltpu.make_async_copy(lat_hbm.at[m, span], raw_ref.at[span, m], sem.at[c, m])

    for c in range(chunks):
        for m in range(members):
            fetch(c, m).start()

    tile = int_ref.shape[1]
    tile_sub = lax.broadcasted_iota(jnp.int32, (tile, LANES), 0)

    def integers(seg, _):
        value = meta_ref[seg, 2 * members :, :].astype(jnp.int32)
        row = value // LANES * (hours * members) + value % members
        int_ref[seg] = jnp.where(tile_sub < 2, value, row)
        return 0

    lax.fori_loop(first, seg_count, integers, 0)
    table = pltpu.make_async_copy(int_ref, table_ref, table_sem)
    table.start()

    def clear(i, _):
        up_ref[i] = jnp.zeros((2 * rows, LANES), jnp.float32)
        return 0

    lax.fori_loop(lev, 2 * lev, clear, 0, unroll=8)

    def turned(values):
        return jnp.concatenate([values] * packs, axis=0).T

    def coefficients(seg, _):
        storage = 0.02 + 0.1 * jax.nn.sigmoid(meta_ref[seg, :members, :])
        weighting = 0.2 * jax.nn.sigmoid(meta_ref[seg, members : 2 * members, :])
        den = storage * (1.0 - weighting) + 0.5
        span = pl.ds(pl.multiple_of(seg * seg_blocks, seg_blocks), seg_blocks)
        now_ref[span, :] = turned((0.5 - storage * weighting) / den)
        back_ref[span, :] = turned((0.5 + storage * weighting) / den)
        carry_ref[span, :] = turned((storage * (1.0 - weighting) - 0.5) / den)
        return 0

    lax.fori_loop(first, seg_count, coefficients, 0)
    for k in range(param_count - 2):
        par_ref[k] = turned(0.2 * prior_ref[:, 2 + k, :])

    group_of = lane // members
    row_group = lax.broadcasted_iota(jnp.int32, (1, LANES), 1) // members

    def pick(pieces, order, where):
        made = pieces[order(0)]
        for q in range(1, packs):
            made = jnp.where(where == q, pieces[order(q)], made)
        return made

    def place_group(tiles, where):
        mixed = [pick(tiles, lambda q, g=g: (g - q) % packs, where) for g in range(packs)]
        mixed = [jnp.broadcast_to(tile, shape) for tile in mixed]
        flat = jnp.concatenate(mixed, axis=0).T
        strips = [flat[q * rows : (q + 1) * rows] for q in range(packs)]
        made = []
        for i in range(packs):
            turn = pick(strips, lambda g, i=i: (g - i) % packs, group_of)
            made.append(pltpu.roll(turn, LANES - i * members, 1) if i else turn)
        return made

    def relayout(group, _):
        base = group * packs
        for h in range(hours):
            tiles = [raw_ref[(base + i) * hours + h] for i in range(packs)]
            for i, tile in enumerate(place_group(tiles, group_of)):
                ready_ref[base + i, h] = tile
        for n, ref in enumerate((pin_ref, pout_ref)):
            tiles = [ref[pl.ds(base + i, 1), :] for i in range(packs)]
            for i, tile in enumerate(place_group(tiles, row_group)):
                ready_ref[base + i, hours + n] = tile
        return 0

    chunk_groups = seg_blocks // packs // chunks
    for c in range(chunks):
        for m in range(members):
            fetch(c, m).wait()
        lax.fori_loop(c * chunk_groups, (c + 1) * chunk_groups, relayout, 0, unroll=4)

    table.wait()

    def sweep(seg, level, parity, own):
        def block(j, _):
            here = level * lev + j
            b = seg * seg_blocks + here
            live = place < table_ref[seg, 1, here]
            now = now_ref[pl.ds(b, 1), :]
            back = back_ref[pl.ds(b, 1), :]
            carry = carry_ref[pl.ds(b, 1), :]
            if own:
                expo = cos_ref[0] * par_ref[0, pl.ds(here, 1), :]
                for k in range(1, cos_ref.shape[0]):
                    expo = expo + cos_ref[k] * par_ref[k, pl.ds(here, 1), :]
                scale = jnp.exp(expo)
                add0 = ready_ref[here, 0] * scale
                add1 = ready_ref[here, 1] * scale
                if level > 0:
                    add0 = add0 + up_ref[parity * lev + j, :rows]
                    add1 = add1 + up_ref[parity * lev + j, rows:]
                in0 = jnp.where(live, add0, 0.0)
                in1 = jnp.where(live, add1, 0.0)
                start = back * ready_ref[here, 2] + carry * ready_ref[here, 3]
                out0 = now * in0 + jnp.where(live, start, 0.0)
            else:
                in0 = jnp.where(live, up_ref[parity * lev + j, :rows], 0.0)
                in1 = jnp.where(live, up_ref[parity * lev + j, rows:], 0.0)
                out0 = now * in0
            out1 = now * in1 + back * in0 + carry * out0
            up_ref[parity * lev + j] = jnp.zeros((2 * rows, LANES), jnp.float32)
            flow_ref[pl.ds(here * 2 * rows, rows), :] = out0
            flow_ref[pl.ds(here * 2 * rows + rows, rows), :] = out1
            target = (1 - parity) * lev + table_ref[seg, 0, here]
            up_ref[target, :rows] += out0
            up_ref[target, rows:] += out1
            return 0

        lax.fori_loop(0, lev, block, 0, unroll=4)

    def observe(seg):
        def part_of(part, _):
            for g in range(LANES):
                row = table_ref[seg, 2 + part, g]
                row_ref[0, g : g + 1, :] = flow_ref[pl.ds(row, 1), :]
                row_ref[1, g : g + 1, :] = flow_ref[pl.ds(row + rows, 1), :]
            slot = meta_ref[seg, pl.ds(2 * members + 2 + part, 1), :].astype(jnp.int32)
            pack = slot % LANES // members
            span = pl.ds(pl.multiple_of(part * LANES, LANES), LANES)
            for h in range(hours):
                turned_rows = row_ref[h].T
                strips = [turned_rows[q * rows : (q + 1) * rows] for q in range(packs)]
                out_ref[seg, h * members : (h + 1) * members, span] = pick(strips, lambda q: q, pack)
            return 0

        lax.fori_loop(0, gauges // LANES, part_of, 0)

    def nothing(seg, _):
        out_ref[seg] = jnp.zeros(out_ref.shape[1:], jnp.float32)
        return 0

    lax.fori_loop(0, first, nothing, 0)
    for level in range(level_count):
        sweep(first, level, level % 2, True)
    observe(first)

    def later(seg, _):
        for level in range(level_count):
            sweep(seg, level, level % 2, False)
        observe(seg)
        return 0

    lax.fori_loop(first + 1, seg_count, later, 0)


def invert_small(d, panel=8):
    size = d.shape[0]
    lane = lax.broadcasted_iota(jnp.int32, d.shape, 1)
    sub = lax.broadcasted_iota(jnp.int32, d.shape, 0)
    for base in range(0, size, panel):
        cols = [jnp.broadcast_to(d[:, base + i : base + i + 1], d.shape) for i in range(panel)]
        for i in range(panel):
            j = base + i
            pivot = cols[i]
            inv = 1.0 / pivot[j : j + 1, :]
            row = jnp.where(lane[:1] == j, 1.0, d[j : j + 1, :]) * inv
            d = jnp.where(sub == j, row, jnp.where(lane == j, 0.0, d) - pivot * row)
            for l in range(i + 1, panel):
                factor = pivot[base + l : base + l + 1, :] * inv
                cols[l] = jnp.where(sub == j, factor, cols[l] - pivot * factor)
    return d


def exact_dot(a, b):
    return jnp.dot(a, b, precision=exact_mode, preferred_element_type=jnp.float32)


def solve_body(n, size, sums_ref, out_ref, a_ref, l_ref):
    total = n * size
    sub = lax.broadcasted_iota(jnp.int32, (total, total), 0)
    lane = lax.broadcasted_iota(jnp.int32, (total, total), 1)
    a_ref[...] = sums_ref[:total, :] + jnp.where(lane == sub, 1.0, 0.0)
    out_ref[...] = sums_ref[total : total + size, :].T
    for k in range(n):
        span = slice(k * size, (k + 1) * size)
        left = (k * size // LANES) * LANES
        inverse = invert_small(a_ref[span, span])
        right = exact_dot(inverse, out_ref[span, :])
        l_ref[...] = a_ref[:, span]
        l_ref[span, :] = jnp.zeros((size, size), jnp.float32)
        column = l_ref[...]
        if k < n - 1:
            top = exact_dot(inverse, a_ref[span, left:])
            a_ref[:, left:] -= exact_dot(column, top)
            a_ref[span, left:] = top
        out_ref[...] -= exact_dot(column, right)
        out_ref[span, :] = right


def inverse_sinh(values):
    return jnp.log(values + jnp.sqrt(values * values + 1.0))


def shards(
    prior_params, lateral_flow, inflow_start, outflow_start, reach_count, downstream,
    gauge_reach, observed, obs_var, obs_noise,
):
    md, param_count, block_dev = prior_params.shape
    hours = lateral_flow.shape[1]
    gauges = gauge_reach.shape[0]
    basins = lax.axis_size("basin")
    n_member = lax.axis_size("member")
    members = md * n_member
    level_count = block_dev // BLK_LEV
    packs = LANES // md
    f32 = jnp.float32

    prior_steps = doubling_bits(n_member)
    held = permuted_step(prior_params[None], "member", prior_steps[0])

    gauge_rows = gauges // block_dev
    extra = -(md * 2 + 2 + gauge_rows) % 8
    meta = jnp.concatenate(
        [
            prior_params[:, 0, :],
            prior_params[:, 1, :],
            downstream.astype(f32)[None],
            reach_count.astype(f32)[None],
            gauge_reach.astype(f32).reshape(-1, block_dev),
            jnp.zeros((extra, block_dev), f32),
        ],
        0,
    )
    meta_all = exchange(meta, "basin", 1)

    modes = param_count - 2
    lane_pos = np.arange(LANES)
    cosine = np.cos(math.pi * np.arange(modes)[:, None] * (lane_pos[None, :] + 0.5) / LANES)
    cosine = np.swapaxes(cosine.reshape(modes, packs, md), 1, 2)
    cosine = jnp.asarray(np.repeat(cosine, md, axis=2), f32)

    lateral = lateral_flow.reshape(md, hours, block_dev, LANES)
    lateral = jnp.swapaxes(lateral, 1, 2).reshape(md, block_dev * hours, LANES)
    held, meta_all = lax.optimization_barrier((held, meta_all))
    for bit in prior_steps[1:-1]:
        held = permuted_step(held, "member", bit)
    basin_idx = lax.axis_index("basin").astype(jnp.int32).reshape(1)
    seg_coef = VMEM((basins * block_dev, LANES), f32)

    parts = pl.pallas_call(
        functools.partial(route_body, basins, level_count, md, gauges, hours, param_count),
        out_shape=jax.ShapeDtypeStruct((basins, 2 * md, gauges), f32),
        in_specs=[smem_spec()] + [vmem_spec()] * 5 + [pl.BlockSpec(memory_space=pl.ANY)],
        out_specs=vmem_spec(),
        scratch_shapes=[
            VMEM((2 * BLK_LEV, 2 * md, LANES), f32),
            VMEM((block_dev * 2 * md, LANES), f32),
            VMEM((hours, LANES, LANES), f32),
            seg_coef,
            seg_coef,
            seg_coef,
            VMEM((modes, block_dev, LANES), f32),
            VMEM((block_dev * hours, md, LANES), f32),
            VMEM((block_dev, hours + 2, md, LANES), f32),
            VMEM((basins, meta.shape[0] - 2 * md, LANES), jnp.int32),
            SMEM((basins, meta.shape[0] - 2 * md, LANES), jnp.int32),
            pltpu.SemaphoreType.DMA((4, md)),
            pltpu.SemaphoreType.DMA,
        ],
        cost_estimate=pl.CostEstimate(
            flops=40_000_000, bytes_accessed=60_000_000, transcendentals=0
        ),
        name="route",
    )(
        basin_idx, meta_all, prior_params, cosine,
        inflow_start.reshape(block_dev, LANES), outflow_start.reshape(block_dev, LANES), lateral,
    )
    parts, held = lax.optimization_barrier((parts, held))
    held = permuted_step(held, "member", prior_steps[-1])
    prior_all = held.reshape(members, param_count * block_dev)
    gathered = observed_gather(parts, hours, 2)
    flat = gathered[0]
    predicted = flat.reshape(md, hours, gauges)
    pred_all = gathered.reshape(members, hours * gauges)

    spread = jnp.sqrt(obs_var).reshape(1, -1)
    spread_root = math.sqrt(members - 1.0)
    noise = jnp.concatenate([obs_noise[:, h] for h in range(hours)], axis=1)
    innovation = (observed.reshape(1, -1) + 2.0 * spread * noise - flat) / (2.0 * spread)
    mean_pred = jnp.sum(pred_all, 0, keepdims=True) / members
    scaled_all = (pred_all - mean_pred) / (spread_root * (2.0 * spread))
    row_count = members + md
    extra = -row_count % (8 * basins)
    both = jnp.concatenate([scaled_all, innovation, jnp.zeros((extra, flat.shape[1]), f32)], 0)
    part = lax.dot_general(
        both, scaled_all, (((1,), (1,)), ((), ())),
        precision=exact_mode, preferred_element_type=f32,
    )
    sums = sum_over(part.reshape(basins, -1, members), "basin", 4).reshape(-1, members)
    gain = pl.pallas_call(
        functools.partial(solve_body, n_member, md),
        out_shape=jax.ShapeDtypeStruct((members, md), f32),
        in_specs=[vmem_spec()],
        out_specs=vmem_spec(),
        scratch_shapes=[VMEM((members, members), f32), VMEM((members, md), f32)],
        cost_estimate=pl.CostEstimate(
            flops=40_000_000, bytes_accessed=60_000_000, transcendentals=0
        ),
        name="solve",
    )(sums)

    mean_prior = jnp.sum(prior_all, 0, keepdims=True) / members
    anomaly = (prior_all - mean_prior) / spread_root
    change = lax.dot_general(
        gain, anomaly, (((0,), (0,)), ((), ())), precision=exact_mode, preferred_element_type=f32
    )
    posterior = prior_params + change.reshape(md, param_count, block_dev)
    return (posterior, predicted)


def solution(mesh):
    return jax.shard_map(
        shards,
        mesh=mesh,
        in_specs=(
            P("member", None, "basin"),
            P("member", None, "basin"),
            P("basin"),
            P("basin"),
            P("basin"),
            P("basin"),
            P("basin"),
            P(None, "basin"),
            P(None, "basin"),
            P("member", None, "basin"),
        ),
        out_specs=(P("member", None, "basin"), P("member", None, "basin")),
        check_vma=False,
    )
```

```python
import functools
import math

import jax
import jax.numpy as jnp
from jax import lax
import numpy as np
from jax.experimental import pallas as pl
from jax.experimental.pallas import tpu as pltpu
from jax.sharding import PartitionSpec as P

LANES = 128
BLK_LEV = 64
exact_mode = lax.Precision.HIGHEST
VMEM = pltpu.VMEM
SMEM = pltpu.SMEM
MESH = pl.DeviceIdType.MESH


def vmem_spec():
    return pl.BlockSpec(memory_space=VMEM)


def smem_spec():
    return pl.BlockSpec(memory_space=SMEM)


def exchange_body(
    n, prior_ref, down_ref, count_ref, gauge_ref, coef_ref, table_ref, send_sem, recv_sem, own_sem
):
    me = lax.axis_index("basin")
    barrier = pltpu.get_barrier_semaphore()
    for i in range(1, n):
        @pl.when(me + i < n)
        def _():
            pl.semaphore_signal(
                barrier, inc=1, device_id={"basin": lax.rem(me + i, n)}, device_id_type=MESH
            )
    @pl.when(me > 0)
    def _():
        pl.semaphore_wait(barrier, me)

    gauge_rows = gauge_ref.shape[0]
    pieces = [
        (prior_ref.at[:, 0:2, :], coef_ref.at[me, :, 0:2, :]),
        (down_ref, table_ref.at[me, 0:1, :]),
        (count_ref, table_ref.at[me, 1:2, :]),
        (gauge_ref, table_ref.at[me, 2 : 2 + gauge_rows, :]),
    ]

    def remote(i, k):
        src, dst = pieces[k]
        return pltpu.make_async_remote_copy(
            src_ref=src, dst_ref=dst,
            send_sem=send_sem.at[i - 1, k], recv_sem=recv_sem.at[i - 1, k],
            device_id={"basin": lax.rem(me - i + n, n)}, device_id_type=MESH,
        )

    for i in range(1, n):
        @pl.when(me - i >= 0)
        def _():
            for k in range(len(pieces)):
                remote(i, k).start()
    own = [pltpu.make_async_copy(src, dst, own_sem.at[k]) for k, (src, dst) in enumerate(pieces)]
    for copy in own:
        copy.start()
    for copy in own:
        copy.wait()
    for i in range(1, n):
        @pl.when(me + i < n)
        def _():
            for k in range(len(pieces)):
                remote(i, k).wait_recv()

        @pl.when(me - i >= 0)
        def _():
            for k in range(len(pieces)):
                remote(i, k).wait_send()


def exchange(prior, down, count, gauge, collective_id):
    n = lax.axis_size("basin")
    return pl.pallas_call(
        functools.partial(exchange_body, n),
        out_shape=(
            jax.ShapeDtypeStruct((n,) + prior.shape, prior.dtype),
            jax.ShapeDtypeStruct((n, 8, LANES), down.dtype),
        ),
        in_specs=[vmem_spec()] * 4,
        out_specs=(vmem_spec(), vmem_spec()),
        scratch_shapes=[
            pltpu.SemaphoreType.DMA((n - 1, 4)),
            pltpu.SemaphoreType.DMA((n - 1, 4)),
            pltpu.SemaphoreType.DMA((4,)),
        ],
        compiler_params=pltpu.CompilerParams(collective_id=collective_id, has_side_effects=True),
        name=f"exchange_{collective_id}",
    )(prior, down, count, gauge)


def doubling_bits(n):
    bits = []
    bit = n // 2
    while bit:
        bits.append(bit)
        bit //= 2
    return bits


def observed_body(
    hours, n_basin, n, x_ref, o_ref, land_ref, part_send, part_recv, send_sem, recv_sem
):
    basin = lax.axis_index("basin")
    me = lax.axis_index("member")
    partners = [me + bit * (1 - 2 * lax.rem(me // bit, 2)) for bit in doubling_bits(n)]
    barrier = pltpu.get_barrier_semaphore()
    for i in range(1, n_basin):
        pl.semaphore_signal(
            barrier, inc=1, device_id={"basin": lax.rem(basin + i, n_basin)}, device_id_type=MESH
        )
    for partner in partners:
        pl.semaphore_signal(barrier, inc=1, device_id={"member": partner}, device_id_type=MESH)
    pl.semaphore_wait(barrier, n_basin - 1 + len(partners))
    parts = []
    for i in range(1, n_basin):
        peer = lax.rem(basin + i, n_basin)
        parts.append(
            pltpu.make_async_remote_copy(
                src_ref=x_ref.at[peer], dst_ref=land_ref.at[i - 1],
                send_sem=part_send.at[i - 1], recv_sem=part_recv.at[i - 1],
                device_id={"basin": peer}, device_id_type=MESH,
            )
        )
    for copy in parts:
        copy.start()
    for copy in parts:
        copy.wait()
    flows = x_ref[basin]
    for i in range(1, n_basin):
        flows = flows + land_ref[i - 1]
    pred = inverse_sinh(flows)
    rows = o_ref.shape[1]
    gauges = x_ref.shape[2]
    for h in range(hours):
        o_ref[0, :, h * gauges : (h + 1) * gauges] = pred[h * rows : (h + 1) * rows]

    copies = {}
    for p in range(n):
        if p:
            copies[p].wait_recv()
        for k, partner in enumerate(partners):
            to = 2**k + p
            if p < 2**k:
                copies[to] = pltpu.make_async_remote_copy(
                    src_ref=o_ref.at[p], dst_ref=o_ref.at[to],
                    send_sem=send_sem.at[to - 1], recv_sem=recv_sem.at[to - 1],
                    device_id={"member": partner}, device_id_type=MESH,
                )
                copies[to].start()
    for p in range(1, n):
        copies[p].wait_send()


def observed_gather(parts, hours, collective_id):
    n = lax.axis_size("member")
    n_basin = lax.axis_size("basin")
    rows, gauges = parts.shape[1] // hours, parts.shape[2]
    return pl.pallas_call(
        functools.partial(observed_body, hours, n_basin, n),
        out_shape=jax.ShapeDtypeStruct((n, rows, hours * gauges), parts.dtype),
        in_specs=[vmem_spec()],
        out_specs=vmem_spec(),
        scratch_shapes=[
            VMEM((n_basin - 1,) + parts.shape[1:], parts.dtype),
            pltpu.SemaphoreType.DMA((n_basin - 1,)),
            pltpu.SemaphoreType.DMA((n_basin - 1,)),
            pltpu.SemaphoreType.DMA((n - 1,)),
            pltpu.SemaphoreType.DMA((n - 1,)),
        ],
        compiler_params=pltpu.CompilerParams(collective_id=collective_id, has_side_effects=True),
        name=f"observed_{collective_id}",
    )(parts)


def sum_body(axis, n, x_ref, o_ref, land_ref, sem1, sem2, sem3, sem4):
    me = lax.axis_index(axis)
    barrier = pltpu.get_barrier_semaphore()
    for i in range(1, n):
        pl.semaphore_signal(
            barrier, inc=1, device_id={axis: lax.rem(me + i, n)}, device_id_type=MESH
        )
    pl.semaphore_wait(barrier, n - 1)
    copies = []
    for i in range(1, n):
        peer = lax.rem(me + i, n)
        copies.append(
            pltpu.make_async_remote_copy(
                src_ref=x_ref.at[peer], dst_ref=land_ref.at[i - 1],
                send_sem=sem1.at[i - 1], recv_sem=sem2.at[i - 1],
                device_id={axis: peer}, device_id_type=MESH,
            )
        )
    for copy in copies:
        copy.start()
    for copy in copies:
        copy.wait()
    total = x_ref[me]
    for i in range(1, n):
        total = total + land_ref[i - 1]
    o_ref[me] = total
    copies = []
    for i in range(1, n):
        copies.append(
            pltpu.make_async_remote_copy(
                src_ref=o_ref.at[me], dst_ref=o_ref.at[me],
                send_sem=sem3.at[i - 1], recv_sem=sem4.at[i - 1],
                device_id={axis: lax.rem(me + i, n)}, device_id_type=MESH,
            )
        )
    for copy in copies:
        copy.start()
    for copy in copies:
        copy.wait()


def sum_over(x, axis, collective_id):
    n = lax.axis_size(axis)
    return pl.pallas_call(
        functools.partial(sum_body, axis, n),
        out_shape=jax.ShapeDtypeStruct(x.shape, x.dtype),
        in_specs=[vmem_spec()],
        out_specs=vmem_spec(),
        scratch_shapes=[VMEM((n - 1,) + x.shape[1:], x.dtype)]
        + [pltpu.SemaphoreType.DMA((n - 1,))] * 4,
        compiler_params=pltpu.CompilerParams(collective_id=collective_id, has_side_effects=True),
        name=f"sum_{collective_id}",
    )(x)


def permuted_step(held, axis, bit):
    n = lax.axis_size(axis)
    other = lax.ppermute(held, axis, [(i, i ^ bit) for i in range(n)])
    return jnp.concatenate([held, other], 0)


def split_two(values):
    high = values.astype(jnp.bfloat16)
    low = (values - high.astype(jnp.float32)).astype(jnp.bfloat16)
    return jnp.concatenate([high, low], axis=1)


def route_body(
    seg_count, level_count, members, gauges, hours, param_count,
    basin_ref, coef_ref, given_ref, prior_ref, cos_ref, pin_ref, pout_ref, lat_hbm,
    out_ref,
    up_ref, flow_ref, row_ref, now_ref, back_ref, carry_ref, par_ref, raw_ref, ready_ref,
    int_ref, table_ref, sem, table_sem,
):
    first = basin_ref[0]
    lev = BLK_LEV
    seg_blocks = level_count * lev
    rows = members
    packs = LANES // members
    shape = (rows, LANES)
    lane = lax.broadcasted_iota(jnp.int32, shape, 1)
    place = (lane // members) * members + lax.broadcasted_iota(jnp.int32, shape, 0)

    chunks = sem.shape[0]
    chunk_rows = seg_blocks * hours // chunks

    def fetch(c, m):
        span = pl.ds(c * chunk_rows, chunk_rows)
        return pltpu.make_async_copy(lat_hbm.at[m, span], raw_ref.at[span, m], sem.at[c, m])

    for c in range(chunks):
        for m in range(members):
            fetch(c, m).start()

    tile = int_ref.shape[1]
    tile_sub = lax.broadcasted_iota(jnp.int32, (tile, LANES), 0)

    def integers(seg, _):
        value = given_ref[seg]
        row = value // LANES * (hours * members) + value % members
        int_ref[seg] = jnp.where(tile_sub < 2, value, row)
        return 0

    lax.fori_loop(first, seg_count, integers, 0)
    table = pltpu.make_async_copy(int_ref, table_ref, table_sem)
    table.start()

    def clear(i, _):
        up_ref[i] = jnp.zeros((2 * rows, LANES), jnp.float32)
        return 0

    lax.fori_loop(lev, 2 * lev, clear, 0, unroll=8)

    def turned(values):
        return jnp.concatenate([values] * packs, axis=0).T

    def coefficients(seg, _):
        storage = 0.02 + 0.1 * jax.nn.sigmoid(coef_ref[seg, :, 0, :])
        weighting = 0.2 * jax.nn.sigmoid(coef_ref[seg, :, 1, :])
        den = storage * (1.0 - weighting) + 0.5
        span = pl.ds(pl.multiple_of(seg * seg_blocks, seg_blocks), seg_blocks)
        now_ref[span, :] = turned((0.5 - storage * weighting) / den)
        back_ref[span, :] = turned((0.5 + storage * weighting) / den)
        carry_ref[span, :] = turned((storage * (1.0 - weighting) - 0.5) / den)
        return 0

    lax.fori_loop(first, seg_count, coefficients, 0)
    for k in range(param_count - 2):
        par_ref[k] = turned(0.2 * prior_ref[:, 2 + k, :])

    group_of = lane // members
    row_group = lax.broadcasted_iota(jnp.int32, (1, LANES), 1) // members

    def pick(pieces, order, where):
        made = pieces[order(0)]
        for q in range(1, packs):
            made = jnp.where(where == q, pieces[order(q)], made)
        return made

    def place_group(tiles, where):
        mixed = [pick(tiles, lambda q, g=g: (g - q) % packs, where) for g in range(packs)]
        mixed = [jnp.broadcast_to(tile, shape) for tile in mixed]
        flat = jnp.concatenate(mixed, axis=0).T
        strips = [flat[q * rows : (q + 1) * rows] for q in range(packs)]
        made = []
        for i in range(packs):
            turn = pick(strips, lambda g, i=i: (g - i) % packs, group_of)
            made.append(pltpu.roll(turn, LANES - i * members, 1) if i else turn)
        return made

    def relayout(group, _):
        base = group * packs
        for h in range(hours):
            tiles = [raw_ref[(base + i) * hours + h] for i in range(packs)]
            for i, tile in enumerate(place_group(tiles, group_of)):
                ready_ref[base + i, h] = tile
        for n, ref in enumerate((pin_ref, pout_ref)):
            tiles = [ref[pl.ds(base + i, 1), :] for i in range(packs)]
            for i, tile in enumerate(place_group(tiles, row_group)):
                ready_ref[base + i, hours + n] = tile
        return 0

    chunk_groups = seg_blocks // packs // chunks
    for c in range(chunks):
        for m in range(members):
            fetch(c, m).wait()
        lax.fori_loop(c * chunk_groups, (c + 1) * chunk_groups, relayout, 0, unroll=4)

    table.wait()

    def sweep(seg, level, parity, own):
        def block(j, _):
            here = level * lev + j
            b = seg * seg_blocks + here
            live = place < table_ref[seg, 1, here]
            now = now_ref[pl.ds(b, 1), :]
            back = back_ref[pl.ds(b, 1), :]
            carry = carry_ref[pl.ds(b, 1), :]
            if own:
                expo = cos_ref[0] * par_ref[0, pl.ds(here, 1), :]
                for k in range(1, cos_ref.shape[0]):
                    expo = expo + cos_ref[k] * par_ref[k, pl.ds(here, 1), :]
                scale = jnp.exp(expo)
                add0 = ready_ref[here, 0] * scale
                add1 = ready_ref[here, 1] * scale
                if level > 0:
                    add0 = add0 + up_ref[parity * lev + j, :rows]
                    add1 = add1 + up_ref[parity * lev + j, rows:]
                in0 = jnp.where(live, add0, 0.0)
                in1 = jnp.where(live, add1, 0.0)
                start = back * ready_ref[here, 2] + carry * ready_ref[here, 3]
                out0 = now * in0 + jnp.where(live, start, 0.0)
            else:
                in0 = jnp.where(live, up_ref[parity * lev + j, :rows], 0.0)
                in1 = jnp.where(live, up_ref[parity * lev + j, rows:], 0.0)
                out0 = now * in0
            out1 = now * in1 + back * in0 + carry * out0
            up_ref[parity * lev + j] = jnp.zeros((2 * rows, LANES), jnp.float32)
            flow_ref[pl.ds(here * 2 * rows, rows), :] = out0
            flow_ref[pl.ds(here * 2 * rows + rows, rows), :] = out1
            target = (1 - parity) * lev + table_ref[seg, 0, here]
            up_ref[target, :rows] += out0
            up_ref[target, rows:] += out1
            return 0

        lax.fori_loop(0, lev, block, 0, unroll=4)

    def observe(seg):
        def part_of(part, _):
            for g in range(LANES):
                row = table_ref[seg, 2 + part, g]
                row_ref[0, g : g + 1, :] = flow_ref[pl.ds(row, 1), :]
                row_ref[1, g : g + 1, :] = flow_ref[pl.ds(row + rows, 1), :]
            slot = given_ref[seg, pl.ds(2 + part, 1), :]
            pack = slot % LANES // members
            span = pl.ds(pl.multiple_of(part * LANES, LANES), LANES)
            for h in range(hours):
                turned_rows = row_ref[h].T
                strips = [turned_rows[q * rows : (q + 1) * rows] for q in range(packs)]
                out_ref[seg, h * members : (h + 1) * members, span] = pick(strips, lambda q: q, pack)
            return 0

        lax.fori_loop(0, gauges // LANES, part_of, 0)

    def nothing(seg, _):
        out_ref[seg] = jnp.zeros(out_ref.shape[1:], jnp.float32)
        return 0

    lax.fori_loop(0, first, nothing, 0)
    for level in range(level_count):
        sweep(first, level, level % 2, True)
    observe(first)

    def later(seg, _):
        for level in range(level_count):
            sweep(seg, level, level % 2, False)
        observe(seg)
        return 0

    lax.fori_loop(first + 1, seg_count, later, 0)


def invert_small(d, panel=8):
    size = d.shape[0]
    lane = lax.broadcasted_iota(jnp.int32, d.shape, 1)
    sub = lax.broadcasted_iota(jnp.int32, d.shape, 0)
    for base in range(0, size, panel):
        cols = [jnp.broadcast_to(d[:, base + i : base + i + 1], d.shape) for i in range(panel)]
        for i in range(panel):
            j = base + i
            pivot = cols[i]
            inv = 1.0 / pivot[j : j + 1, :]
            row = jnp.where(lane[:1] == j, 1.0, d[j : j + 1, :]) * inv
            d = jnp.where(sub == j, row, jnp.where(lane == j, 0.0, d) - pivot * row)
            for l in range(i + 1, panel):
                factor = pivot[base + l : base + l + 1, :] * inv
                cols[l] = jnp.where(sub == j, factor, cols[l] - pivot * factor)
    return d


def exact_dot(a, b):
    return jnp.dot(a, b, precision=exact_mode, preferred_element_type=jnp.float32)


def solve_body(n, size, sums_ref, out_ref, a_ref, l_ref):
    total = n * size
    sub = lax.broadcasted_iota(jnp.int32, (total, total), 0)
    lane = lax.broadcasted_iota(jnp.int32, (total, total), 1)
    a_ref[...] = sums_ref[:total, :] + jnp.where(lane == sub, 1.0, 0.0)
    out_ref[...] = sums_ref[total : total + size, :].T
    for k in range(n):
        span = slice(k * size, (k + 1) * size)
        left = (k * size // LANES) * LANES
        inverse = invert_small(a_ref[span, span])
        right = exact_dot(inverse, out_ref[span, :])
        l_ref[...] = a_ref[:, span]
        l_ref[span, :] = jnp.zeros((size, size), jnp.float32)
        column = l_ref[...]
        if k < n - 1:
            top = exact_dot(inverse, a_ref[span, left:])
            a_ref[:, left:] -= exact_dot(column, top)
            a_ref[span, left:] = top
        out_ref[...] -= exact_dot(column, right)
        out_ref[span, :] = right


def inverse_sinh(values):
    return jnp.log(values + jnp.sqrt(values * values + 1.0))


def shards(
    prior_params, lateral_flow, inflow_start, outflow_start, reach_count, downstream,
    gauge_reach, observed, obs_var, obs_noise,
):
    md, param_count, block_dev = prior_params.shape
    hours = lateral_flow.shape[1]
    gauges = gauge_reach.shape[0]
    basins = lax.axis_size("basin")
    n_member = lax.axis_size("member")
    members = md * n_member
    level_count = block_dev // BLK_LEV
    packs = LANES // md
    f32 = jnp.float32

    prior_steps = doubling_bits(n_member)
    held = permuted_step(prior_params[None], "member", prior_steps[0])

    coef_all, table_all = exchange(
        prior_params, downstream.reshape(1, block_dev), reach_count.reshape(1, block_dev),
        gauge_reach.reshape(-1, block_dev), 1,
    )

    modes = param_count - 2
    lane_pos = np.arange(LANES)
    cosine = np.cos(math.pi * np.arange(modes)[:, None] * (lane_pos[None, :] + 0.5) / LANES)
    cosine = np.swapaxes(cosine.reshape(modes, packs, md), 1, 2)
    cosine = jnp.asarray(np.repeat(cosine, md, axis=2), f32)

    lateral = lateral_flow.reshape(md, hours, block_dev, LANES)
    lateral = jnp.swapaxes(lateral, 1, 2).reshape(md, block_dev * hours, LANES)
    held, coef_all = lax.optimization_barrier((held, coef_all))
    for bit in prior_steps[1:-1]:
        held = permuted_step(held, "member", bit)
    basin_idx = lax.axis_index("basin").astype(jnp.int32).reshape(1)
    seg_coef = VMEM((basins * block_dev, LANES), f32)

    parts = pl.pallas_call(
        functools.partial(route_body, basins, level_count, md, gauges, hours, param_count),
        out_shape=jax.ShapeDtypeStruct((basins, 2 * md, gauges), f32),
        in_specs=[smem_spec()] + [vmem_spec()] * 6 + [pl.BlockSpec(memory_space=pl.ANY)],
        out_specs=vmem_spec(),
        scratch_shapes=[
            VMEM((2 * BLK_LEV, 2 * md, LANES), f32),
            VMEM((block_dev * 2 * md, LANES), f32),
            VMEM((hours, LANES, LANES), f32),
            seg_coef,
            seg_coef,
            seg_coef,
            VMEM((modes, block_dev, LANES), f32),
            VMEM((block_dev * hours, md, LANES), f32),
            VMEM((block_dev, hours + 2, md, LANES), f32),
            VMEM(table_all.shape, jnp.int32),
            SMEM(table_all.shape, jnp.int32),
            pltpu.SemaphoreType.DMA((4, md)),
            pltpu.SemaphoreType.DMA,
        ],
        cost_estimate=pl.CostEstimate(
            flops=40_000_000, bytes_accessed=60_000_000, transcendentals=0
        ),
        name="route",
    )(
        basin_idx, coef_all, table_all, prior_params, cosine,
        inflow_start.reshape(block_dev, LANES), outflow_start.reshape(block_dev, LANES), lateral,
    )
    parts, held = lax.optimization_barrier((parts, held))
    held = permuted_step(held, "member", prior_steps[-1])
    prior_all = held.reshape(members, param_count * block_dev)
    gathered = observed_gather(parts, hours, 2)
    flat = gathered[0]
    predicted = flat.reshape(md, hours, gauges)
    pred_all = gathered.reshape(members, hours * gauges)

    spread = jnp.sqrt(obs_var).reshape(1, -1)
    spread_root = math.sqrt(members - 1.0)
    noise = jnp.concatenate([obs_noise[:, h] for h in range(hours)], axis=1)
    innovation = (observed.reshape(1, -1) + 2.0 * spread * noise - flat) / (2.0 * spread)
    mean_pred = jnp.sum(pred_all, 0, keepdims=True) / members
    scaled_all = (pred_all - mean_pred) / (spread_root * (2.0 * spread))
    row_count = members + md
    extra = -row_count % (8 * basins)
    both = jnp.concatenate([scaled_all, innovation, jnp.zeros((extra, flat.shape[1]), f32)], 0)
    part = lax.dot_general(
        both, scaled_all, (((1,), (1,)), ((), ())),
        precision=exact_mode, preferred_element_type=f32,
    )
    sums = sum_over(part.reshape(basins, -1, members), "basin", 4).reshape(-1, members)
    gain = pl.pallas_call(
        functools.partial(solve_body, n_member, md),
        out_shape=jax.ShapeDtypeStruct((members, md), f32),
        in_specs=[vmem_spec()],
        out_specs=vmem_spec(),
        scratch_shapes=[VMEM((members, members), f32), VMEM((members, md), f32)],
        cost_estimate=pl.CostEstimate(
            flops=40_000_000, bytes_accessed=60_000_000, transcendentals=0
        ),
        name="solve",
    )(sums)

    mean_prior = jnp.sum(prior_all, 0, keepdims=True) / members
    anomaly = (prior_all - mean_prior) / spread_root
    change = lax.dot_general(
        gain, anomaly, (((0,), (0,)), ((), ())), precision=exact_mode, preferred_element_type=f32
    )
    posterior = prior_params + change.reshape(md, param_count, block_dev)
    return (posterior, predicted)


def solution(mesh):
    return jax.shard_map(
        shards,
        mesh=mesh,
        in_specs=(
            P("member", None, "basin"),
            P("member", None, "basin"),
            P("basin"),
            P("basin"),
            P("basin"),
            P("basin"),
            P("basin"),
            P(None, "basin"),
            P(None, "basin"),
            P("member", None, "basin"),
        ),
        out_specs=(P("member", None, "basin"), P("member", None, "basin")),
        check_vma=False,
    )
```

```python
import functools
import math

import jax
import jax.numpy as jnp
from jax import lax
import numpy as np
from jax.experimental import pallas as pl
from jax.experimental.pallas import tpu as pltpu
from jax.sharding import PartitionSpec as P

LANES = 128
BLK_LEV = 64
exact_mode = lax.Precision.HIGHEST
VMEM = pltpu.VMEM
SMEM = pltpu.SMEM
MESH = pl.DeviceIdType.MESH


def vmem_spec():
    return pl.BlockSpec(memory_space=VMEM)


def smem_spec():
    return pl.BlockSpec(memory_space=SMEM)


def exchange_body(
    n, prior_ref, down_ref, count_ref, gauge_ref, coef_ref, table_ref, send_sem, recv_sem, own_sem
):
    me = lax.axis_index("basin")
    barrier = pltpu.get_barrier_semaphore()
    for i in range(1, n):
        @pl.when(me + i < n)
        def _():
            pl.semaphore_signal(
                barrier, inc=1, device_id={"basin": lax.rem(me + i, n)}, device_id_type=MESH
            )
    @pl.when(me > 0)
    def _():
        pl.semaphore_wait(barrier, me)

    gauge_rows = gauge_ref.shape[0]
    pieces = [
        (prior_ref.at[:, 0:2, :], coef_ref.at[me, :, 0:2, :]),
        (down_ref, table_ref.at[me, 0:1, :]),
        (count_ref, table_ref.at[me, 1:2, :]),
        (gauge_ref, table_ref.at[me, 2 : 2 + gauge_rows, :]),
    ]

    def remote(i, k):
        src, dst = pieces[k]
        return pltpu.make_async_remote_copy(
            src_ref=src, dst_ref=dst,
            send_sem=send_sem.at[i - 1, k], recv_sem=recv_sem.at[i - 1, k],
            device_id={"basin": lax.rem(me - i + n, n)}, device_id_type=MESH,
        )

    for i in range(1, n):
        @pl.when(me - i >= 0)
        def _():
            for k in range(len(pieces)):
                remote(i, k).start()
    own = [pltpu.make_async_copy(src, dst, own_sem.at[k]) for k, (src, dst) in enumerate(pieces)]
    for copy in own:
        copy.start()
    for copy in own:
        copy.wait()
    for i in range(1, n):
        @pl.when(me + i < n)
        def _():
            for k in range(len(pieces)):
                remote(i, k).wait_recv()

        @pl.when(me - i >= 0)
        def _():
            for k in range(len(pieces)):
                remote(i, k).wait_send()


def exchange(prior, down, count, gauge, collective_id):
    n = lax.axis_size("basin")
    return pl.pallas_call(
        functools.partial(exchange_body, n),
        out_shape=(
            jax.ShapeDtypeStruct((n,) + prior.shape, prior.dtype),
            jax.ShapeDtypeStruct((n, 8, LANES), down.dtype),
        ),
        in_specs=[vmem_spec()] * 4,
        out_specs=(vmem_spec(), vmem_spec()),
        scratch_shapes=[
            pltpu.SemaphoreType.DMA((n - 1, 4)),
            pltpu.SemaphoreType.DMA((n - 1, 4)),
            pltpu.SemaphoreType.DMA((4,)),
        ],
        compiler_params=pltpu.CompilerParams(collective_id=collective_id, has_side_effects=True),
        name=f"exchange_{collective_id}",
    )(prior, down, count, gauge)


def doubling_bits(n):
    bits = []
    bit = n // 2
    while bit:
        bits.append(bit)
        bit //= 2
    return bits


def assimilate_body(
    hours, n_basin, n, padded,
    x_ref, obs_ref, var_ref, noise_ref, pred_ref, sums_ref,
    all_ref, land_ref, high_ref, low_ref, part_ref, land_g, land_c,
    part_send, part_recv, send_sem, recv_sem,
    gram_send, gram_recv, cross_send, cross_recv,
    gram_out, gram_in, cross_out, cross_in, side_out, side_in,
):
    basin = lax.axis_index("basin")
    me = lax.axis_index("member")
    rows = all_ref.shape[1]
    gauges = x_ref.shape[2]
    members = n * rows
    partners = [me + bit * (1 - 2 * lax.rem(me // bit, 2)) for bit in doubling_bits(n)]
    barrier = pltpu.get_barrier_semaphore()
    for i in range(1, n_basin):
        @pl.when(basin - i >= 0)
        def _():
            pl.semaphore_signal(
                barrier, inc=1, device_id={"basin": lax.rem(basin - i + n_basin, n_basin)},
                device_id_type=MESH,
            )
    for partner in partners:
        pl.semaphore_signal(barrier, inc=1, device_id={"member": partner}, device_id_type=MESH)
    pl.semaphore_wait(barrier, n_basin - 1 - basin + len(partners))

    def part_copy(i):
        peer = lax.rem(basin + i, n_basin)
        return pltpu.make_async_remote_copy(
            src_ref=x_ref.at[peer], dst_ref=land_ref.at[i - 1],
            send_sem=part_send.at[i - 1], recv_sem=part_recv.at[i - 1],
            device_id={"basin": peer}, device_id_type=MESH,
        )

    for i in range(n_basin - 1, 0, -1):
        @pl.when(basin + i < n_basin)
        def _():
            part_copy(i).start()

    spread = 2.0 * jnp.sqrt(var_ref[...])
    for h in range(hours):
        span = slice(h * gauges, (h + 1) * gauges)
        all_ref[0, :, span] = x_ref[basin, h * rows : (h + 1) * rows, :]
    for i in range(1, n_basin):
        @pl.when(basin - i >= 0)
        def _():
            part_copy(i).wait_recv()
            for h in range(hours):
                span = slice(h * gauges, (h + 1) * gauges)
                all_ref[0, :, span] += land_ref[i - 1, h * rows : (h + 1) * rows, :]
    all_ref[0] = inverse_sinh(all_ref[0])

    copies = {}
    for p in range(n):
        if p:
            copies[p].wait_recv()
        for k, partner in enumerate(partners):
            to = 2**k + p
            if p < 2**k:
                copies[to] = pltpu.make_async_remote_copy(
                    src_ref=all_ref.at[p], dst_ref=all_ref.at[to],
                    send_sem=send_sem.at[to - 1], recv_sem=recv_sem.at[to - 1],
                    device_id={"member": partner}, device_id_type=MESH,
                )
                copies[to].start()
        if p == 0:
            for h in range(hours):
                span = slice(h * gauges, (h + 1) * gauges)
                wide = spread[h : h + 1, :]
                flow = all_ref[0, :, span]
                pred_ref[:, h, :] = flow
                away = (obs_ref[h : h + 1, :] + wide * noise_ref[:, h, :] - flow) / wide
                high = away.astype(jnp.bfloat16)
                high_ref[members : members + rows, span] = high
                low_ref[members : members + rows, span] = (
                    away - high.astype(jnp.float32)
                ).astype(jnp.bfloat16)
    for p in range(1, n):
        copies[p].wait_send()
    for i in range(1, n_basin):
        @pl.when(basin + i < n_basin)
        def _():
            part_copy(i).wait_send()

    for h in range(hours):
        span = slice(h * gauges, (h + 1) * gauges)
        total = all_ref[0, :, span]
        for p in range(1, n):
            total = total + all_ref[p, :, span]
        mean = jnp.sum(total, 0, keepdims=True) / members
        over = math.sqrt(members - 1.0) * spread[h : h + 1, :]
        for p in range(n):
            scaled = (all_ref[p, :, span] - mean) / over
            high = scaled.astype(jnp.bfloat16)
            high_ref[p * rows : (p + 1) * rows, span] = high
            low_ref[p * rows : (p + 1) * rows, span] = (
                scaled - high.astype(jnp.float32)
            ).astype(jnp.bfloat16)

    def product(a, b):
        return lax.dot_general(
            a, b, (((1,), (1,)), ((), ())), preferred_element_type=jnp.float32
        )

    used = members + rows
    part_ref[:used, :] = (
        product(high_ref[...], high_ref[:members, :])
        + product(high_ref[...], low_ref[:members, :])
        + product(low_ref[...], high_ref[:members, :])
    )
    if padded > rows:
        part_ref[used:, :] = jnp.zeros((padded - rows, members), jnp.float32)

    piece_g = members // (2 * n_basin)
    piece_c = padded // n_basin

    def gram_rows(side, which):
        return pl.ds(pl.multiple_of((side * n_basin + which) * piece_g, piece_g), piece_g)

    def cross_rows(which):
        return pl.ds(pl.multiple_of(members + which * piece_c, piece_c), piece_c)

    first = []
    for i in range(1, n_basin):
        peer = lax.rem(basin + i, n_basin)
        for src, dst, out_sem, in_sem in (
            (part_ref.at[gram_rows(0, peer)], land_g.at[i - 1], gram_send, gram_recv),
            (part_ref.at[cross_rows(peer)], land_c.at[i - 1], cross_send, cross_recv),
        ):
            first.append(
                pltpu.make_async_remote_copy(
                    src_ref=src, dst_ref=dst,
                    send_sem=out_sem.at[i - 1], recv_sem=in_sem.at[i - 1],
                    device_id={"basin": peer}, device_id_type=MESH,
                )
            )
    for copy in first:
        copy.start()
    for copy in first:
        copy.wait_recv()
    total_g = part_ref[gram_rows(0, basin), :]
    total_c = part_ref[cross_rows(basin), :]
    for i in range(1, n_basin):
        total_g = total_g + land_g[i - 1]
        total_c = total_c + land_c[i - 1]
    sums_ref[gram_rows(0, basin), :] = total_g
    sums_ref[cross_rows(basin), :] = total_c

    def spread_copy(span, i, out_sem, in_sem):
        return pltpu.make_async_remote_copy(
            src_ref=sums_ref.at[span], dst_ref=sums_ref.at[span],
            send_sem=out_sem.at[i - 1], recv_sem=in_sem.at[i - 1],
            device_id={"basin": lax.rem(basin + i, n_basin)}, device_id_type=MESH,
        )

    half = members // 2

    def side_copies(i):
        which = lax.rem(basin - i + n_basin, n_basin)
        return [
            pltpu.make_async_remote_copy(
                src_ref=sums_ref.at[gram_rows(0, which), a * half : (a + 1) * half],
                dst_ref=sums_ref.at[gram_rows(1, which), (1 - a) * half : (2 - a) * half],
                send_sem=side_out.at[i, a], recv_sem=side_in.at[i, a],
                device_id={"member": partners[-1]}, device_id_type=MESH,
            )
            for a in range(2)
        ]

    second = []
    for i in range(1, n_basin):
        second.append(
            (spread_copy(gram_rows(0, basin), i, gram_out, gram_in),
             spread_copy(cross_rows(basin), i, cross_out, cross_in))
        )
    for pair in second:
        for copy in pair:
            copy.start()
    sides = side_copies(0)
    for copy in sides:
        copy.start()
    for i in range(1, n_basin):
        second[i - 1][0].wait_recv()
        passed = side_copies(i)
        for copy in passed:
            copy.start()
        sides = sides + passed
    for pair in second:
        pair[1].wait_recv()
    for copy in sides:
        copy.wait_recv()
    for copy in first + sides:
        copy.wait_send()
    for pair in second:
        for copy in pair:
            copy.wait_send()


def assimilate(parts, observed, obs_var, obs_noise, collective_id):
    n = lax.axis_size("member")
    nb = lax.axis_size("basin")
    rows, hours, gauges = obs_noise.shape
    width = hours * gauges
    members = n * rows
    padded = rows + -rows % (8 * nb)
    f32, bf16 = jnp.float32, jnp.bfloat16
    dma = pltpu.SemaphoreType.DMA
    return pl.pallas_call(
        functools.partial(assimilate_body, hours, nb, n, padded),
        out_shape=(
            jax.ShapeDtypeStruct((rows, hours, gauges), f32),
            jax.ShapeDtypeStruct((members + padded, members), f32),
        ),
        in_specs=[vmem_spec()] * 4,
        out_specs=(vmem_spec(), vmem_spec()),
        scratch_shapes=[
            VMEM((n, rows, width), f32),
            VMEM((nb - 1,) + parts.shape[1:], f32),
            VMEM((members + rows, width), bf16),
            VMEM((members + rows, width), bf16),
            VMEM((members + padded, members), f32),
            VMEM((nb - 1, members // (2 * nb), members), f32),
            VMEM((nb - 1, padded // nb, members), f32),
        ]
        + [dma((nb - 1,))] * 2
        + [dma((n - 1,))] * 2
        + [dma((nb - 1,))] * 8
        + [dma((nb, 2))] * 2,
        compiler_params=pltpu.CompilerParams(collective_id=collective_id, has_side_effects=True),
        name=f"assimilate_{collective_id}",
    )(parts, observed, obs_var, obs_noise)


def permuted_step(held, axis, bit):
    n = lax.axis_size(axis)
    other = lax.ppermute(held, axis, [(i, i ^ bit) for i in range(n)])
    return jnp.concatenate([held, other], 0)


def split_two(values):
    high = values.astype(jnp.bfloat16)
    low = (values - high.astype(jnp.float32)).astype(jnp.bfloat16)
    return jnp.concatenate([high, low], axis=1)


def route_body(
    seg_count, level_count, members, gauges, hours, param_count,
    basin_ref, coef_ref, given_ref, prior_ref, cos_ref, pin_ref, pout_ref, lat_hbm,
    out_ref,
    up_ref, flow_ref, row_ref, now_ref, back_ref, carry_ref, par_ref, raw_ref, ready_ref,
    int_ref, table_ref, sem, table_sem,
):
    first = basin_ref[0]
    lev = BLK_LEV
    seg_blocks = level_count * lev
    rows = members
    packs = LANES // members
    shape = (rows, LANES)
    lane = lax.broadcasted_iota(jnp.int32, shape, 1)
    place = (lane // members) * members + lax.broadcasted_iota(jnp.int32, shape, 0)

    chunks = sem.shape[0]
    chunk_rows = seg_blocks * hours // chunks

    def fetch(c, m):
        span = pl.ds(c * chunk_rows, chunk_rows)
        return pltpu.make_async_copy(lat_hbm.at[m, span], raw_ref.at[span, m], sem.at[c, m])

    for c in range(chunks):
        for m in range(members):
            fetch(c, m).start()

    tile = int_ref.shape[1]
    tile_sub = lax.broadcasted_iota(jnp.int32, (tile, LANES), 0)

    def integers(seg, _):
        value = given_ref[seg]
        row = value // LANES * (hours * members) + value % members
        int_ref[seg] = jnp.where(tile_sub < 2, value, row)
        return 0

    lax.fori_loop(first, seg_count, integers, 0)
    table = pltpu.make_async_copy(int_ref, table_ref, table_sem)
    table.start()

    def clear(i, _):
        up_ref[i] = jnp.zeros((2 * rows, LANES), jnp.float32)
        return 0

    lax.fori_loop(lev, 2 * lev, clear, 0, unroll=8)

    def turned(values):
        return jnp.concatenate([values] * packs, axis=0).T

    def coefficients(seg, _):
        storage = 0.02 + 0.1 * jax.nn.sigmoid(coef_ref[seg, :, 0, :])
        weighting = 0.2 * jax.nn.sigmoid(coef_ref[seg, :, 1, :])
        den = storage * (1.0 - weighting) + 0.5
        span = pl.ds(pl.multiple_of(seg * seg_blocks, seg_blocks), seg_blocks)
        now_ref[span, :] = turned((0.5 - storage * weighting) / den)
        back_ref[span, :] = turned((0.5 + storage * weighting) / den)
        carry_ref[span, :] = turned((storage * (1.0 - weighting) - 0.5) / den)
        return 0

    lax.fori_loop(first, seg_count, coefficients, 0)
    for k in range(param_count - 2):
        par_ref[k] = turned(0.2 * prior_ref[:, 2 + k, :])

    group_of = lane // members
    row_group = lax.broadcasted_iota(jnp.int32, (1, LANES), 1) // members

    def pick(pieces, order, where):
        made = pieces[order(0)]
        for q in range(1, packs):
            made = jnp.where(where == q, pieces[order(q)], made)
        return made

    def place_group(tiles, where):
        mixed = [pick(tiles, lambda q, g=g: (g - q) % packs, where) for g in range(packs)]
        mixed = [jnp.broadcast_to(tile, shape) for tile in mixed]
        flat = jnp.concatenate(mixed, axis=0).T
        strips = [flat[q * rows : (q + 1) * rows] for q in range(packs)]
        made = []
        for i in range(packs):
            turn = pick(strips, lambda g, i=i: (g - i) % packs, group_of)
            made.append(pltpu.roll(turn, LANES - i * members, 1) if i else turn)
        return made

    def relayout(group, _):
        base = group * packs
        for h in range(hours):
            tiles = [raw_ref[(base + i) * hours + h] for i in range(packs)]
            for i, tile in enumerate(place_group(tiles, group_of)):
                ready_ref[base + i, h] = tile
        for n, ref in enumerate((pin_ref, pout_ref)):
            tiles = [ref[pl.ds(base + i, 1), :] for i in range(packs)]
            for i, tile in enumerate(place_group(tiles, row_group)):
                ready_ref[base + i, hours + n] = tile
        return 0

    chunk_groups = seg_blocks // packs // chunks
    for c in range(chunks):
        for m in range(members):
            fetch(c, m).wait()
        lax.fori_loop(c * chunk_groups, (c + 1) * chunk_groups, relayout, 0, unroll=4)

    table.wait()

    def sweep(seg, level, parity, own):
        def block(j, _):
            here = level * lev + j
            b = seg * seg_blocks + here
            live = place < table_ref[seg, 1, here]
            now = now_ref[pl.ds(b, 1), :]
            back = back_ref[pl.ds(b, 1), :]
            carry = carry_ref[pl.ds(b, 1), :]
            if own:
                expo = cos_ref[0] * par_ref[0, pl.ds(here, 1), :]
                for k in range(1, cos_ref.shape[0]):
                    expo = expo + cos_ref[k] * par_ref[k, pl.ds(here, 1), :]
                scale = jnp.exp(expo)
                add0 = ready_ref[here, 0] * scale
                add1 = ready_ref[here, 1] * scale
                if level > 0:
                    add0 = add0 + up_ref[parity * lev + j, :rows]
                    add1 = add1 + up_ref[parity * lev + j, rows:]
                in0 = jnp.where(live, add0, 0.0)
                in1 = jnp.where(live, add1, 0.0)
                start = back * ready_ref[here, 2] + carry * ready_ref[here, 3]
                out0 = now * in0 + jnp.where(live, start, 0.0)
            else:
                in0 = jnp.where(live, up_ref[parity * lev + j, :rows], 0.0)
                in1 = jnp.where(live, up_ref[parity * lev + j, rows:], 0.0)
                out0 = now * in0
            out1 = now * in1 + back * in0 + carry * out0
            up_ref[parity * lev + j] = jnp.zeros((2 * rows, LANES), jnp.float32)
            flow_ref[pl.ds(here * 2 * rows, rows), :] = out0
            flow_ref[pl.ds(here * 2 * rows + rows, rows), :] = out1
            target = (1 - parity) * lev + table_ref[seg, 0, here]
            up_ref[target, :rows] += out0
            up_ref[target, rows:] += out1
            return 0

        lax.fori_loop(0, lev, block, 0, unroll=4)

    def observe(seg):
        def part_of(part, _):
            for g in range(LANES):
                row = table_ref[seg, 2 + part, g]
                row_ref[0, g : g + 1, :] = flow_ref[pl.ds(row, 1), :]
                row_ref[1, g : g + 1, :] = flow_ref[pl.ds(row + rows, 1), :]
            slot = given_ref[seg, pl.ds(2 + part, 1), :]
            pack = slot % LANES // members
            span = pl.ds(pl.multiple_of(part * LANES, LANES), LANES)
            for h in range(hours):
                turned_rows = row_ref[h].T
                strips = [turned_rows[q * rows : (q + 1) * rows] for q in range(packs)]
                out_ref[seg, h * members : (h + 1) * members, span] = pick(strips, lambda q: q, pack)
            return 0

        lax.fori_loop(0, gauges // LANES, part_of, 0)

    def nothing(seg, _):
        out_ref[seg] = jnp.zeros(out_ref.shape[1:], jnp.float32)
        return 0

    lax.fori_loop(0, first, nothing, 0)
    for level in range(level_count):
        sweep(first, level, level % 2, True)
    observe(first)

    def later(seg, _):
        for level in range(level_count):
            sweep(seg, level, level % 2, False)
        observe(seg)
        return 0

    lax.fori_loop(first + 1, seg_count, later, 0)


def invert_small(d, panel=8):
    size = d.shape[0]
    lane = lax.broadcasted_iota(jnp.int32, d.shape, 1)
    sub = lax.broadcasted_iota(jnp.int32, d.shape, 0)
    for base in range(0, size, panel):
        cols = [jnp.broadcast_to(d[:, base + i : base + i + 1], d.shape) for i in range(panel)]
        for i in range(panel):
            j = base + i
            pivot = cols[i]
            inv = 1.0 / pivot[j : j + 1, :]
            row = jnp.where(lane[:1] == j, 1.0, d[j : j + 1, :]) * inv
            d = jnp.where(sub == j, row, jnp.where(lane == j, 0.0, d) - pivot * row)
            for l in range(i + 1, panel):
                factor = pivot[base + l : base + l + 1, :] * inv
                cols[l] = jnp.where(sub == j, factor, cols[l] - pivot * factor)
    return d


def exact_dot(a, b):
    return jnp.dot(a, b, precision=exact_mode, preferred_element_type=jnp.float32)


def solve_body(n, size, sums_ref, out_ref, a_ref, l_ref):
    total = n * size
    sub = lax.broadcasted_iota(jnp.int32, (total, total), 0)
    lane = lax.broadcasted_iota(jnp.int32, (total, total), 1)
    a_ref[...] = sums_ref[:total, :] + jnp.where(lane == sub, 1.0, 0.0)
    out_ref[...] = sums_ref[total : total + size, :].T
    for k in range(n):
        span = slice(k * size, (k + 1) * size)
        left = (k * size // LANES) * LANES
        inverse = invert_small(a_ref[span, span])
        right = exact_dot(inverse, out_ref[span, :])
        l_ref[...] = a_ref[:, span]
        l_ref[span, :] = jnp.zeros((size, size), jnp.float32)
        column = l_ref[...]
        if k < n - 1:
            top = exact_dot(inverse, a_ref[span, left:])
            a_ref[:, left:] -= exact_dot(column, top)
            a_ref[span, left:] = top
        out_ref[...] -= exact_dot(column, right)
        out_ref[span, :] = right


def inverse_sinh(values):
    return jnp.log(values + jnp.sqrt(values * values + 1.0))


def shards(
    prior_params, lateral_flow, inflow_start, outflow_start, reach_count, downstream,
    gauge_reach, observed, obs_var, obs_noise,
):
    md, param_count, block_dev = prior_params.shape
    hours = lateral_flow.shape[1]
    gauges = gauge_reach.shape[0]
    basins = lax.axis_size("basin")
    n_member = lax.axis_size("member")
    members = md * n_member
    level_count = block_dev // BLK_LEV
    packs = LANES // md
    f32 = jnp.float32

    prior_steps = doubling_bits(n_member)
    held = permuted_step(prior_params[None], "member", prior_steps[0])

    coef_all, table_all = exchange(
        prior_params, downstream.reshape(1, block_dev), reach_count.reshape(1, block_dev),
        gauge_reach.reshape(-1, block_dev), 1,
    )

    modes = param_count - 2
    lane_pos = np.arange(LANES)
    cosine = np.cos(math.pi * np.arange(modes)[:, None] * (lane_pos[None, :] + 0.5) / LANES)
    cosine = np.swapaxes(cosine.reshape(modes, packs, md), 1, 2)
    cosine = jnp.asarray(np.repeat(cosine, md, axis=2), f32)

    lateral = lateral_flow.reshape(md, hours, block_dev, LANES)
    lateral = jnp.swapaxes(lateral, 1, 2).reshape(md, block_dev * hours, LANES)
    held, coef_all = lax.optimization_barrier((held, coef_all))
    for bit in prior_steps[1:-1]:
        held = permuted_step(held, "member", bit)
    basin_idx = lax.axis_index("basin").astype(jnp.int32).reshape(1)
    seg_coef = VMEM((basins * block_dev, LANES), f32)

    parts = pl.pallas_call(
        functools.partial(route_body, basins, level_count, md, gauges, hours, param_count),
        out_shape=jax.ShapeDtypeStruct((basins, 2 * md, gauges), f32),
        in_specs=[smem_spec()] + [vmem_spec()] * 6 + [pl.BlockSpec(memory_space=pl.ANY)],
        out_specs=vmem_spec(),
        scratch_shapes=[
            VMEM((2 * BLK_LEV, 2 * md, LANES), f32),
            VMEM((block_dev * 2 * md, LANES), f32),
            VMEM((hours, LANES, LANES), f32),
            seg_coef,
            seg_coef,
            seg_coef,
            VMEM((modes, block_dev, LANES), f32),
            VMEM((block_dev * hours, md, LANES), f32),
            VMEM((block_dev, hours + 2, md, LANES), f32),
            VMEM(table_all.shape, jnp.int32),
            SMEM(table_all.shape, jnp.int32),
            pltpu.SemaphoreType.DMA((4, md)),
            pltpu.SemaphoreType.DMA,
        ],
        cost_estimate=pl.CostEstimate(
            flops=40_000_000, bytes_accessed=60_000_000, transcendentals=0
        ),
        name="route",
    )(
        basin_idx, coef_all, table_all, prior_params, cosine,
        inflow_start.reshape(block_dev, LANES), outflow_start.reshape(block_dev, LANES), lateral,
    )
    parts, held = lax.optimization_barrier((parts, held))
    held = permuted_step(held, "member", prior_steps[-1])
    prior_all = held.reshape(members, param_count * block_dev)
    predicted, sums = assimilate(parts, observed, obs_var, obs_noise, 2)
    spread_root = math.sqrt(members - 1.0)
    gain = pl.pallas_call(
        functools.partial(solve_body, n_member, md),
        out_shape=jax.ShapeDtypeStruct((members, md), f32),
        in_specs=[vmem_spec()],
        out_specs=vmem_spec(),
        scratch_shapes=[VMEM((members, members), f32), VMEM((members, md), f32)],
        cost_estimate=pl.CostEstimate(
            flops=40_000_000, bytes_accessed=60_000_000, transcendentals=0
        ),
        name="solve",
    )(sums)

    mean_prior = jnp.sum(prior_all, 0, keepdims=True) / members
    anomaly = (prior_all - mean_prior) / spread_root
    change = lax.dot_general(
        gain, anomaly, (((0,), (0,)), ((), ())), precision=exact_mode, preferred_element_type=f32
    )
    posterior = prior_params + change.reshape(md, param_count, block_dev)
    return (posterior, predicted)


def solution(mesh):
    return jax.shard_map(
        shards,
        mesh=mesh,
        in_specs=(
            P("member", None, "basin"),
            P("member", None, "basin"),
            P("basin"),
            P("basin"),
            P("basin"),
            P("basin"),
            P("basin"),
            P(None, "basin"),
            P(None, "basin"),
            P("member", None, "basin"),
        ),
        out_specs=(P("member", None, "basin"), P("member", None, "basin")),
        check_vma=False,
    )
```

```python
import functools
import math

import jax
import jax.numpy as jnp
from jax import lax
import numpy as np
from jax.experimental import pallas as pl
from jax.experimental.pallas import tpu as pltpu
from jax.sharding import PartitionSpec as P

LANES = 128
BLK_LEV = 64
exact_mode = lax.Precision.HIGHEST
VMEM = pltpu.VMEM
SMEM = pltpu.SMEM
MESH = pl.DeviceIdType.MESH


def vmem_spec():
    return pl.BlockSpec(memory_space=VMEM)


def smem_spec():
    return pl.BlockSpec(memory_space=SMEM)


def exchange_body(
    n, prior_ref, down_ref, count_ref, gauge_ref, coef_ref, table_ref, send_sem, recv_sem, own_sem
):
    me = lax.axis_index("basin")
    barrier = pltpu.get_barrier_semaphore()
    for i in range(1, n):
        @pl.when(me + i < n)
        def _():
            pl.semaphore_signal(
                barrier, inc=1, device_id={"basin": lax.rem(me + i, n)}, device_id_type=MESH
            )
    @pl.when(me > 0)
    def _():
        pl.semaphore_wait(barrier, me)

    gauge_rows = gauge_ref.shape[0]
    pieces = [
        (prior_ref.at[:, 0:2, :], coef_ref.at[me, :, 0:2, :]),
        (down_ref, table_ref.at[me, 0:1, :]),
        (count_ref, table_ref.at[me, 1:2, :]),
        (gauge_ref, table_ref.at[me, 2 : 2 + gauge_rows, :]),
    ]

    def remote(i, k):
        src, dst = pieces[k]
        return pltpu.make_async_remote_copy(
            src_ref=src, dst_ref=dst,
            send_sem=send_sem.at[i - 1, k], recv_sem=recv_sem.at[i - 1, k],
            device_id={"basin": lax.rem(me - i + n, n)}, device_id_type=MESH,
        )

    for i in range(1, n):
        @pl.when(me - i >= 0)
        def _():
            for k in range(len(pieces)):
                remote(i, k).start()
    own = [pltpu.make_async_copy(src, dst, own_sem.at[k]) for k, (src, dst) in enumerate(pieces)]
    for copy in own:
        copy.start()
    for copy in own:
        copy.wait()
    for i in range(1, n):
        @pl.when(me + i < n)
        def _():
            for k in range(len(pieces)):
                remote(i, k).wait_recv()

        @pl.when(me - i >= 0)
        def _():
            for k in range(len(pieces)):
                remote(i, k).wait_send()


def exchange(prior, down, count, gauge, collective_id):
    n = lax.axis_size("basin")
    return pl.pallas_call(
        functools.partial(exchange_body, n),
        out_shape=(
            jax.ShapeDtypeStruct((n,) + prior.shape, prior.dtype),
            jax.ShapeDtypeStruct((n, 8, LANES), down.dtype),
        ),
        in_specs=[vmem_spec()] * 4,
        out_specs=(vmem_spec(), vmem_spec()),
        scratch_shapes=[
            pltpu.SemaphoreType.DMA((n - 1, 4)),
            pltpu.SemaphoreType.DMA((n - 1, 4)),
            pltpu.SemaphoreType.DMA((4,)),
        ],
        compiler_params=pltpu.CompilerParams(collective_id=collective_id, has_side_effects=True),
        name=f"exchange_{collective_id}",
    )(prior, down, count, gauge)


def doubling_bits(n):
    bits = []
    bit = n // 2
    while bit:
        bits.append(bit)
        bit //= 2
    return bits


def assimilate_body(
    hours, n_basin, n, padded,
    x_ref, obs_ref, var_ref, noise_ref, pred_ref, sums_ref,
    all_ref, land_ref, high_ref, low_ref, part_ref, land_g, land_c,
    part_send, part_recv, send_sem, recv_sem,
    gram_send, gram_recv, cross_send, cross_recv,
    gram_out, gram_in, cross_out, cross_in, side_out, side_in,
):
    basin = lax.axis_index("basin")
    me = lax.axis_index("member")
    rows = all_ref.shape[2]
    gauges = x_ref.shape[2]
    members = n * rows
    partners = [me + bit * (1 - 2 * lax.rem(me // bit, 2)) for bit in doubling_bits(n)]
    barrier = pltpu.get_barrier_semaphore()
    for i in range(1, n_basin):
        @pl.when(basin - i >= 0)
        def _():
            pl.semaphore_signal(
                barrier, inc=1, device_id={"basin": lax.rem(basin - i + n_basin, n_basin)},
                device_id_type=MESH,
            )
    for partner in partners:
        pl.semaphore_signal(barrier, inc=1, device_id={"member": partner}, device_id_type=MESH)
    pl.semaphore_wait(barrier, n_basin - 1 - basin + len(partners))

    def part_copy(i, h):
        peer = lax.rem(basin + i, n_basin)
        span = slice(h * rows, (h + 1) * rows)
        return pltpu.make_async_remote_copy(
            src_ref=x_ref.at[peer, span], dst_ref=land_ref.at[i - 1, span],
            send_sem=part_send.at[i - 1, h], recv_sem=part_recv.at[i - 1, h],
            device_id={"basin": peer}, device_id_type=MESH,
        )

    for h in range(hours):
        for i in range(n_basin - 1, 0, -1):
            @pl.when(basin + i < n_basin)
            def _():
                part_copy(i, h).start()

    copies = {}

    def pass_on(p, h):
        for k, partner in enumerate(partners):
            to = 2**k + p
            if p < 2**k:
                copies[to, h] = pltpu.make_async_remote_copy(
                    src_ref=all_ref.at[h, p], dst_ref=all_ref.at[h, to],
                    send_sem=send_sem.at[to - 1, h], recv_sem=recv_sem.at[to - 1, h],
                    device_id={"member": partner}, device_id_type=MESH,
                )
                copies[to, h].start()

    spread = 2.0 * jnp.sqrt(var_ref[...])
    for h in range(hours):
        all_ref[h, 0] = x_ref[basin, h * rows : (h + 1) * rows, :]
        for i in range(1, n_basin):
            @pl.when(basin - i >= 0)
            def _():
                part_copy(i, h).wait_recv()
                all_ref[h, 0] += land_ref[i - 1, h * rows : (h + 1) * rows, :]
        all_ref[h, 0] = inverse_sinh(all_ref[h, 0])
        pass_on(0, h)
    for h in range(hours):
        span = slice(h * gauges, (h + 1) * gauges)
        wide = spread[h : h + 1, :]
        flow = all_ref[h, 0]
        pred_ref[:, h, :] = flow
        away = (obs_ref[h : h + 1, :] + wide * noise_ref[:, h, :] - flow) / wide
        high = away.astype(jnp.bfloat16)
        high_ref[members : members + rows, span] = high
        low_ref[members : members + rows, span] = (
            away - high.astype(jnp.float32)
        ).astype(jnp.bfloat16)
    for p in range(1, n):
        for h in range(hours):
            copies[p, h].wait_recv()
            pass_on(p, h)

    for h in range(hours):
        span = slice(h * gauges, (h + 1) * gauges)
        total = all_ref[h, 0]
        for p in range(1, n):
            total = total + all_ref[h, p]
        mean = jnp.sum(total, 0, keepdims=True) / members
        over = math.sqrt(members - 1.0) * spread[h : h + 1, :]
        for p in range(n):
            scaled = (all_ref[h, p] - mean) / over
            high = scaled.astype(jnp.bfloat16)
            high_ref[p * rows : (p + 1) * rows, span] = high
            low_ref[p * rows : (p + 1) * rows, span] = (
                scaled - high.astype(jnp.float32)
            ).astype(jnp.bfloat16)

    def product(a, b):
        return lax.dot_general(
            a, b, (((1,), (1,)), ((), ())), preferred_element_type=jnp.float32
        )

    used = members + rows
    part_ref[:used, :] = (
        product(high_ref[...], high_ref[:members, :])
        + product(high_ref[...], low_ref[:members, :])
        + product(low_ref[...], high_ref[:members, :])
    )
    if padded > rows:
        part_ref[used:, :] = jnp.zeros((padded - rows, members), jnp.float32)

    piece_g = members // (2 * n_basin)
    piece_c = padded // n_basin

    def gram_rows(side, which):
        return pl.ds(pl.multiple_of((side * n_basin + which) * piece_g, piece_g), piece_g)

    def cross_rows(which):
        return pl.ds(pl.multiple_of(members + which * piece_c, piece_c), piece_c)

    first = []
    for i in range(1, n_basin):
        peer = lax.rem(basin + i, n_basin)
        for src, dst, out_sem, in_sem in (
            (part_ref.at[gram_rows(0, peer)], land_g.at[i - 1], gram_send, gram_recv),
            (part_ref.at[cross_rows(peer)], land_c.at[i - 1], cross_send, cross_recv),
        ):
            first.append(
                pltpu.make_async_remote_copy(
                    src_ref=src, dst_ref=dst,
                    send_sem=out_sem.at[i - 1], recv_sem=in_sem.at[i - 1],
                    device_id={"basin": peer}, device_id_type=MESH,
                )
            )
    for copy in first:
        copy.start()
    for copy in first:
        copy.wait_recv()
    total_g = part_ref[gram_rows(0, basin), :]
    total_c = part_ref[cross_rows(basin), :]
    for i in range(1, n_basin):
        total_g = total_g + land_g[i - 1]
        total_c = total_c + land_c[i - 1]
    sums_ref[gram_rows(0, basin), :] = total_g
    sums_ref[cross_rows(basin), :] = total_c

    def spread_copy(span, i, out_sem, in_sem):
        return pltpu.make_async_remote_copy(
            src_ref=sums_ref.at[span], dst_ref=sums_ref.at[span],
            send_sem=out_sem.at[i - 1], recv_sem=in_sem.at[i - 1],
            device_id={"basin": lax.rem(basin + i, n_basin)}, device_id_type=MESH,
        )

    half = members // 2

    def side_copies(i):
        which = lax.rem(basin - i + n_basin, n_basin)
        return [
            pltpu.make_async_remote_copy(
                src_ref=sums_ref.at[gram_rows(0, which), a * half : (a + 1) * half],
                dst_ref=sums_ref.at[gram_rows(1, which), (1 - a) * half : (2 - a) * half],
                send_sem=side_out.at[i, a], recv_sem=side_in.at[i, a],
                device_id={"member": partners[-1]}, device_id_type=MESH,
            )
            for a in range(2)
        ]

    second = []
    for i in range(1, n_basin):
        second.append(
            (spread_copy(gram_rows(0, basin), i, gram_out, gram_in),
             spread_copy(cross_rows(basin), i, cross_out, cross_in))
        )
    for pair in second:
        for copy in pair:
            copy.start()
    sides = side_copies(0)
    for copy in sides:
        copy.start()
    for i in range(1, n_basin):
        second[i - 1][0].wait_recv()
        passed = side_copies(i)
        for copy in passed:
            copy.start()
        sides = sides + passed
    for pair in second:
        pair[1].wait_recv()
    for copy in sides:
        copy.wait_recv()
    for copy in list(copies.values()) + first + sides:
        copy.wait_send()
    for h in range(hours):
        for i in range(1, n_basin):
            @pl.when(basin + i < n_basin)
            def _():
                part_copy(i, h).wait_send()
    for pair in second:
        for copy in pair:
            copy.wait_send()


def assimilate(parts, observed, obs_var, obs_noise, collective_id):
    n = lax.axis_size("member")
    nb = lax.axis_size("basin")
    rows, hours, gauges = obs_noise.shape
    width = hours * gauges
    members = n * rows
    padded = rows + -rows % (8 * nb)
    f32, bf16 = jnp.float32, jnp.bfloat16
    dma = pltpu.SemaphoreType.DMA
    return pl.pallas_call(
        functools.partial(assimilate_body, hours, nb, n, padded),
        out_shape=(
            jax.ShapeDtypeStruct((rows, hours, gauges), f32),
            jax.ShapeDtypeStruct((members + padded, members), f32),
        ),
        in_specs=[vmem_spec()] * 4,
        out_specs=(vmem_spec(), vmem_spec()),
        scratch_shapes=[
            VMEM((hours, n, rows, gauges), f32),
            VMEM((nb - 1,) + parts.shape[1:], f32),
            VMEM((members + rows, width), bf16),
            VMEM((members + rows, width), bf16),
            VMEM((members + padded, members), f32),
            VMEM((nb - 1, members // (2 * nb), members), f32),
            VMEM((nb - 1, padded // nb, members), f32),
        ]
        + [dma((nb - 1, hours))] * 2
        + [dma((n - 1, hours))] * 2
        + [dma((nb - 1,))] * 8
        + [dma((nb, 2))] * 2,
        compiler_params=pltpu.CompilerParams(collective_id=collective_id, has_side_effects=True),
        name=f"assimilate_{collective_id}",
    )(parts, observed, obs_var, obs_noise)


def permuted_step(held, axis, bit):
    n = lax.axis_size(axis)
    other = lax.ppermute(held, axis, [(i, i ^ bit) for i in range(n)])
    return jnp.concatenate([held, other], 0)


def split_two(values):
    high = values.astype(jnp.bfloat16)
    low = (values - high.astype(jnp.float32)).astype(jnp.bfloat16)
    return jnp.concatenate([high, low], axis=1)


def route_body(
    seg_count, level_count, members, gauges, hours, param_count,
    basin_ref, coef_ref, given_ref, prior_ref, cos_ref, pin_ref, pout_ref, lat_hbm,
    out_ref,
    up_ref, flow_ref, row_ref, now_ref, back_ref, carry_ref, par_ref, raw_ref, ready_ref,
    int_ref, table_ref, sem, table_sem,
):
    first = basin_ref[0]
    lev = BLK_LEV
    seg_blocks = level_count * lev
    rows = members
    packs = LANES // members
    shape = (rows, LANES)
    lane = lax.broadcasted_iota(jnp.int32, shape, 1)
    place = (lane // members) * members + lax.broadcasted_iota(jnp.int32, shape, 0)

    chunks = sem.shape[0]
    chunk_rows = seg_blocks * hours // chunks

    def fetch(c, m):
        span = pl.ds(c * chunk_rows, chunk_rows)
        return pltpu.make_async_copy(lat_hbm.at[m, span], raw_ref.at[span, m], sem.at[c, m])

    for c in range(chunks):
        for m in range(members):
            fetch(c, m).start()

    tile = int_ref.shape[1]
    tile_sub = lax.broadcasted_iota(jnp.int32, (tile, LANES), 0)

    def integers(seg, _):
        value = given_ref[seg]
        row = value // LANES * (hours * members) + value % members
        int_ref[seg] = jnp.where(tile_sub < 2, value, row)
        return 0

    lax.fori_loop(first, seg_count, integers, 0)
    table = pltpu.make_async_copy(int_ref, table_ref, table_sem)
    table.start()

    def clear(i, _):
        up_ref[i] = jnp.zeros((2 * rows, LANES), jnp.float32)
        return 0

    lax.fori_loop(lev, 2 * lev, clear, 0, unroll=8)

    def turned(values):
        return jnp.concatenate([values] * packs, axis=0).T

    def coefficients(seg, _):
        storage = 0.02 + 0.1 * jax.nn.sigmoid(coef_ref[seg, :, 0, :])
        weighting = 0.2 * jax.nn.sigmoid(coef_ref[seg, :, 1, :])
        den = storage * (1.0 - weighting) + 0.5
        span = pl.ds(pl.multiple_of(seg * seg_blocks, seg_blocks), seg_blocks)
        now_ref[span, :] = turned((0.5 - storage * weighting) / den)
        back_ref[span, :] = turned((0.5 + storage * weighting) / den)
        carry_ref[span, :] = turned((storage * (1.0 - weighting) - 0.5) / den)
        return 0

    lax.fori_loop(first, seg_count, coefficients, 0)
    for k in range(param_count - 2):
        par_ref[k] = turned(0.2 * prior_ref[:, 2 + k, :])

    group_of = lane // members
    row_group = lax.broadcasted_iota(jnp.int32, (1, LANES), 1) // members

    def pick(pieces, order, where):
        made = pieces[order(0)]
        for q in range(1, packs):
            made = jnp.where(where == q, pieces[order(q)], made)
        return made

    def place_group(tiles, where):
        mixed = [pick(tiles, lambda q, g=g: (g - q) % packs, where) for g in range(packs)]
        mixed = [jnp.broadcast_to(tile, shape) for tile in mixed]
        flat = jnp.concatenate(mixed, axis=0).T
        strips = [flat[q * rows : (q + 1) * rows] for q in range(packs)]
        made = []
        for i in range(packs):
            turn = pick(strips, lambda g, i=i: (g - i) % packs, group_of)
            made.append(pltpu.roll(turn, LANES - i * members, 1) if i else turn)
        return made

    def relayout(group, _):
        base = group * packs
        for h in range(hours):
            tiles = [raw_ref[(base + i) * hours + h] for i in range(packs)]
            for i, tile in enumerate(place_group(tiles, group_of)):
                ready_ref[base + i, h] = tile
        for n, ref in enumerate((pin_ref, pout_ref)):
            tiles = [ref[pl.ds(base + i, 1), :] for i in range(packs)]
            for i, tile in enumerate(place_group(tiles, row_group)):
                ready_ref[base + i, hours + n] = tile
        return 0

    chunk_groups = seg_blocks // packs // chunks
    for c in range(chunks):
        for m in range(members):
            fetch(c, m).wait()
        lax.fori_loop(c * chunk_groups, (c + 1) * chunk_groups, relayout, 0, unroll=4)

    table.wait()

    def sweep(seg, level, parity, own):
        def block(j, _):
            here = level * lev + j
            b = seg * seg_blocks + here
            live = place < table_ref[seg, 1, here]
            now = now_ref[pl.ds(b, 1), :]
            back = back_ref[pl.ds(b, 1), :]
            carry = carry_ref[pl.ds(b, 1), :]
            if own:
                expo = cos_ref[0] * par_ref[0, pl.ds(here, 1), :]
                for k in range(1, cos_ref.shape[0]):
                    expo = expo + cos_ref[k] * par_ref[k, pl.ds(here, 1), :]
                scale = jnp.exp(expo)
                add0 = ready_ref[here, 0] * scale
                add1 = ready_ref[here, 1] * scale
                if level > 0:
                    add0 = add0 + up_ref[parity * lev + j, :rows]
                    add1 = add1 + up_ref[parity * lev + j, rows:]
                in0 = jnp.where(live, add0, 0.0)
                in1 = jnp.where(live, add1, 0.0)
                start = back * ready_ref[here, 2] + carry * ready_ref[here, 3]
                out0 = now * in0 + jnp.where(live, start, 0.0)
            else:
                in0 = jnp.where(live, up_ref[parity * lev + j, :rows], 0.0)
                in1 = jnp.where(live, up_ref[parity * lev + j, rows:], 0.0)
                out0 = now * in0
            out1 = now * in1 + back * in0 + carry * out0
            up_ref[parity * lev + j] = jnp.zeros((2 * rows, LANES), jnp.float32)
            flow_ref[pl.ds(here * 2 * rows, rows), :] = out0
            flow_ref[pl.ds(here * 2 * rows + rows, rows), :] = out1
            target = (1 - parity) * lev + table_ref[seg, 0, here]
            up_ref[target, :rows] += out0
            up_ref[target, rows:] += out1
            return 0

        lax.fori_loop(0, lev, block, 0, unroll=4)

    def observe(seg):
        def part_of(part, _):
            for g in range(LANES):
                row = table_ref[seg, 2 + part, g]
                row_ref[0, g : g + 1, :] = flow_ref[pl.ds(row, 1), :]
                row_ref[1, g : g + 1, :] = flow_ref[pl.ds(row + rows, 1), :]
            slot = given_ref[seg, pl.ds(2 + part, 1), :]
            pack = slot % LANES // members
            span = pl.ds(pl.multiple_of(part * LANES, LANES), LANES)
            for h in range(hours):
                turned_rows = row_ref[h].T
                strips = [turned_rows[q * rows : (q + 1) * rows] for q in range(packs)]
                out_ref[seg, h * members : (h + 1) * members, span] = pick(strips, lambda q: q, pack)
            return 0

        lax.fori_loop(0, gauges // LANES, part_of, 0)

    def nothing(seg, _):
        out_ref[seg] = jnp.zeros(out_ref.shape[1:], jnp.float32)
        return 0

    lax.fori_loop(0, first, nothing, 0)
    for level in range(level_count):
        sweep(first, level, level % 2, True)
    observe(first)

    def later(seg, _):
        for level in range(level_count):
            sweep(seg, level, level % 2, False)
        observe(seg)
        return 0

    lax.fori_loop(first + 1, seg_count, later, 0)


def invert_small(d, panel=8):
    size = d.shape[0]
    lane = lax.broadcasted_iota(jnp.int32, d.shape, 1)
    sub = lax.broadcasted_iota(jnp.int32, d.shape, 0)
    for base in range(0, size, panel):
        cols = [jnp.broadcast_to(d[:, base + i : base + i + 1], d.shape) for i in range(panel)]
        for i in range(panel):
            j = base + i
            pivot = cols[i]
            inv = 1.0 / pivot[j : j + 1, :]
            row = jnp.where(lane[:1] == j, 1.0, d[j : j + 1, :]) * inv
            d = jnp.where(sub == j, row, jnp.where(lane == j, 0.0, d) - pivot * row)
            for l in range(i + 1, panel):
                factor = pivot[base + l : base + l + 1, :] * inv
                cols[l] = jnp.where(sub == j, factor, cols[l] - pivot * factor)
    return d


def exact_dot(a, b):
    return jnp.dot(a, b, precision=exact_mode, preferred_element_type=jnp.float32)


def solve_body(n, size, sums_ref, out_ref, a_ref, l_ref):
    total = n * size
    sub = lax.broadcasted_iota(jnp.int32, (total, total), 0)
    lane = lax.broadcasted_iota(jnp.int32, (total, total), 1)
    a_ref[...] = sums_ref[:total, :] + jnp.where(lane == sub, 1.0, 0.0)
    out_ref[...] = sums_ref[total : total + size, :].T
    for k in range(n):
        span = slice(k * size, (k + 1) * size)
        left = (k * size // LANES) * LANES
        inverse = invert_small(a_ref[span, span])
        right = exact_dot(inverse, out_ref[span, :])
        l_ref[...] = a_ref[:, span]
        l_ref[span, :] = jnp.zeros((size, size), jnp.float32)
        column = l_ref[...]
        if k < n - 1:
            top = exact_dot(inverse, a_ref[span, left:])
            a_ref[:, left:] -= exact_dot(column, top)
            a_ref[span, left:] = top
        out_ref[...] -= exact_dot(column, right)
        out_ref[span, :] = right


def inverse_sinh(values):
    return jnp.log(values + jnp.sqrt(values * values + 1.0))


def shards(
    prior_params, lateral_flow, inflow_start, outflow_start, reach_count, downstream,
    gauge_reach, observed, obs_var, obs_noise,
):
    md, param_count, block_dev = prior_params.shape
    hours = lateral_flow.shape[1]
    gauges = gauge_reach.shape[0]
    basins = lax.axis_size("basin")
    n_member = lax.axis_size("member")
    members = md * n_member
    level_count = block_dev // BLK_LEV
    packs = LANES // md
    f32 = jnp.float32

    prior_steps = doubling_bits(n_member)
    held = permuted_step(prior_params[None], "member", prior_steps[0])

    coef_all, table_all = exchange(
        prior_params, downstream.reshape(1, block_dev), reach_count.reshape(1, block_dev),
        gauge_reach.reshape(-1, block_dev), 1,
    )

    modes = param_count - 2
    lane_pos = np.arange(LANES)
    cosine = np.cos(math.pi * np.arange(modes)[:, None] * (lane_pos[None, :] + 0.5) / LANES)
    cosine = np.swapaxes(cosine.reshape(modes, packs, md), 1, 2)
    cosine = jnp.asarray(np.repeat(cosine, md, axis=2), f32)

    lateral = lateral_flow.reshape(md, hours, block_dev, LANES)
    lateral = jnp.swapaxes(lateral, 1, 2).reshape(md, block_dev * hours, LANES)
    held, coef_all = lax.optimization_barrier((held, coef_all))
    for bit in prior_steps[1:-1]:
        held = permuted_step(held, "member", bit)
    basin_idx = lax.axis_index("basin").astype(jnp.int32).reshape(1)
    seg_coef = VMEM((basins * block_dev, LANES), f32)

    parts = pl.pallas_call(
        functools.partial(route_body, basins, level_count, md, gauges, hours, param_count),
        out_shape=jax.ShapeDtypeStruct((basins, 2 * md, gauges), f32),
        in_specs=[smem_spec()] + [vmem_spec()] * 6 + [pl.BlockSpec(memory_space=pl.ANY)],
        out_specs=vmem_spec(),
        scratch_shapes=[
            VMEM((2 * BLK_LEV, 2 * md, LANES), f32),
            VMEM((block_dev * 2 * md, LANES), f32),
            VMEM((hours, LANES, LANES), f32),
            seg_coef,
            seg_coef,
            seg_coef,
            VMEM((modes, block_dev, LANES), f32),
            VMEM((block_dev * hours, md, LANES), f32),
            VMEM((block_dev, hours + 2, md, LANES), f32),
            VMEM(table_all.shape, jnp.int32),
            SMEM(table_all.shape, jnp.int32),
            pltpu.SemaphoreType.DMA((4, md)),
            pltpu.SemaphoreType.DMA,
        ],
        cost_estimate=pl.CostEstimate(
            flops=40_000_000, bytes_accessed=60_000_000, transcendentals=0
        ),
        name="route",
    )(
        basin_idx, coef_all, table_all, prior_params, cosine,
        inflow_start.reshape(block_dev, LANES), outflow_start.reshape(block_dev, LANES), lateral,
    )
    parts, held = lax.optimization_barrier((parts, held))
    held = permuted_step(held, "member", prior_steps[-1])
    prior_all = held.reshape(members, param_count * block_dev)
    predicted, sums = assimilate(parts, observed, obs_var, obs_noise, 2)
    spread_root = math.sqrt(members - 1.0)
    gain = pl.pallas_call(
        functools.partial(solve_body, n_member, md),
        out_shape=jax.ShapeDtypeStruct((members, md), f32),
        in_specs=[vmem_spec()],
        out_specs=vmem_spec(),
        scratch_shapes=[VMEM((members, members), f32), VMEM((members, md), f32)],
        cost_estimate=pl.CostEstimate(
            flops=40_000_000, bytes_accessed=60_000_000, transcendentals=0
        ),
        name="solve",
    )(sums)

    mean_prior = jnp.sum(prior_all, 0, keepdims=True) / members
    anomaly = (prior_all - mean_prior) / spread_root
    change = lax.dot_general(
        gain, anomaly, (((0,), (0,)), ((), ())), precision=exact_mode, preferred_element_type=f32
    )
    posterior = prior_params + change.reshape(md, param_count, block_dev)
    return (posterior, predicted)


def solution(mesh):
    return jax.shard_map(
        shards,
        mesh=mesh,
        in_specs=(
            P("member", None, "basin"),
            P("member", None, "basin"),
            P("basin"),
            P("basin"),
            P("basin"),
            P("basin"),
            P("basin"),
            P(None, "basin"),
            P(None, "basin"),
            P("member", None, "basin"),
        ),
        out_specs=(P("member", None, "basin"), P("member", None, "basin")),
        check_vma=False,
    )
```

```python
import functools
import math

import jax
import jax.numpy as jnp
from jax import lax
import numpy as np
from jax.experimental import pallas as pl
from jax.experimental.pallas import tpu as pltpu
from jax.sharding import PartitionSpec as P

LANES = 128
BLK_LEV = 64
exact_mode = lax.Precision.HIGHEST
VMEM = pltpu.VMEM
SMEM = pltpu.SMEM
MESH = pl.DeviceIdType.MESH


def vmem_spec():
    return pl.BlockSpec(memory_space=VMEM)


def smem_spec():
    return pl.BlockSpec(memory_space=SMEM)


def exchange_body(
    n, prior_ref, down_ref, count_ref, gauge_ref, coef_ref, table_ref, send_sem, recv_sem, own_sem
):
    me = lax.axis_index("basin")
    barrier = pltpu.get_barrier_semaphore()
    for i in range(1, n):
        @pl.when(me + i < n)
        def _():
            pl.semaphore_signal(
                barrier, inc=1, device_id={"basin": lax.rem(me + i, n)}, device_id_type=MESH
            )
    @pl.when(me > 0)
    def _():
        pl.semaphore_wait(barrier, me)

    gauge_rows = gauge_ref.shape[0]
    pieces = [
        (prior_ref.at[:, 0:2, :], coef_ref.at[me, :, 0:2, :]),
        (down_ref, table_ref.at[me, 0:1, :]),
        (count_ref, table_ref.at[me, 1:2, :]),
        (gauge_ref, table_ref.at[me, 2 : 2 + gauge_rows, :]),
    ]

    def remote(i, k):
        src, dst = pieces[k]
        return pltpu.make_async_remote_copy(
            src_ref=src, dst_ref=dst,
            send_sem=send_sem.at[i - 1, k], recv_sem=recv_sem.at[i - 1, k],
            device_id={"basin": lax.rem(me - i + n, n)}, device_id_type=MESH,
        )

    for i in range(1, n):
        @pl.when(me - i >= 0)
        def _():
            for k in range(len(pieces)):
                remote(i, k).start()
    own = [pltpu.make_async_copy(src, dst, own_sem.at[k]) for k, (src, dst) in enumerate(pieces)]
    for copy in own:
        copy.start()
    for copy in own:
        copy.wait()
    for i in range(1, n):
        @pl.when(me + i < n)
        def _():
            for k in range(len(pieces)):
                remote(i, k).wait_recv()

        @pl.when(me - i >= 0)
        def _():
            for k in range(len(pieces)):
                remote(i, k).wait_send()


def exchange(prior, down, count, gauge, collective_id):
    n = lax.axis_size("basin")
    return pl.pallas_call(
        functools.partial(exchange_body, n),
        out_shape=(
            jax.ShapeDtypeStruct((n,) + prior.shape, prior.dtype),
            jax.ShapeDtypeStruct((n, 8, LANES), down.dtype),
        ),
        in_specs=[vmem_spec()] * 4,
        out_specs=(vmem_spec(), vmem_spec()),
        scratch_shapes=[
            pltpu.SemaphoreType.DMA((n - 1, 4)),
            pltpu.SemaphoreType.DMA((n - 1, 4)),
            pltpu.SemaphoreType.DMA((4,)),
        ],
        compiler_params=pltpu.CompilerParams(collective_id=collective_id, has_side_effects=True),
        name=f"exchange_{collective_id}",
    )(prior, down, count, gauge)


def doubling_bits(n):
    bits = []
    bit = n // 2
    while bit:
        bits.append(bit)
        bit //= 2
    return bits


def assimilate_body(
    hours, n_basin, n, padded,
    x_ref, obs_ref, var_ref, noise_ref, pred_ref, sums_ref,
    all_ref, land_ref, high_ref, low_ref, part_ref, land_g, land_c,
    part_send, part_recv, send_sem, recv_sem,
    gram_send, gram_recv, cross_send, cross_recv,
    gram_out, gram_in, cross_out, cross_in, side_out, side_in,
):
    basin = lax.axis_index("basin")
    me = lax.axis_index("member")
    rows = all_ref.shape[2]
    chunks, width = all_ref.shape[0], all_ref.shape[3]
    splits = chunks // hours
    members = n * rows
    partners = [me + bit * (1 - 2 * lax.rem(me // bit, 2)) for bit in doubling_bits(n)]
    barrier = pltpu.get_barrier_semaphore()
    for i in range(1, n_basin):
        @pl.when(basin - i >= 0)
        def _():
            pl.semaphore_signal(
                barrier, inc=1, device_id={"basin": lax.rem(basin - i + n_basin, n_basin)},
                device_id_type=MESH,
            )
    for partner in partners:
        pl.semaphore_signal(barrier, inc=1, device_id={"member": partner}, device_id_type=MESH)
    pl.semaphore_wait(barrier, n_basin - 1 - basin + len(partners))

    def place(h):
        hour, split = h // splits, h % splits
        return slice(hour * rows, (hour + 1) * rows), slice(split * width, (split + 1) * width)

    def part_copy(i, h):
        peer = lax.rem(basin + i, n_basin)
        return pltpu.make_async_remote_copy(
            src_ref=x_ref.at[(peer,) + place(h)], dst_ref=land_ref.at[i - 1, h],
            send_sem=part_send.at[i - 1, h], recv_sem=part_recv.at[i - 1, h],
            device_id={"basin": peer}, device_id_type=MESH,
        )

    for h in range(chunks):
        for i in range(n_basin - 1, 0, -1):
            @pl.when(basin + i < n_basin)
            def _():
                part_copy(i, h).start()

    copies = {}

    def pass_on(p, h):
        for k, partner in enumerate(partners):
            to = 2**k + p
            if p < 2**k:
                copies[to, h] = pltpu.make_async_remote_copy(
                    src_ref=all_ref.at[h, p], dst_ref=all_ref.at[h, to],
                    send_sem=send_sem.at[to - 1, h], recv_sem=recv_sem.at[to - 1, h],
                    device_id={"member": partner}, device_id_type=MESH,
                )
                copies[to, h].start()

    spread = 2.0 * jnp.sqrt(var_ref[...])
    for h in range(chunks):
        all_ref[h, 0] = x_ref[(basin,) + place(h)]
        for i in range(1, n_basin):
            @pl.when(basin - i >= 0)
            def _():
                part_copy(i, h).wait_recv()
                all_ref[h, 0] += land_ref[i - 1, h]
        all_ref[h, 0] = inverse_sinh(all_ref[h, 0])
        pass_on(0, h)
    for h in range(chunks):
        span = slice(h * width, (h + 1) * width)
        hour, cols = h // splits, place(h)[1]
        wide = spread[hour : hour + 1, cols]
        flow = all_ref[h, 0]
        pred_ref[:, hour, cols] = flow
        away = (obs_ref[hour : hour + 1, cols] + wide * noise_ref[:, hour, cols] - flow) / wide
        high = away.astype(jnp.bfloat16)
        high_ref[members : members + rows, span] = high
        low_ref[members : members + rows, span] = (
            away - high.astype(jnp.float32)
        ).astype(jnp.bfloat16)
    for p in range(1, n):
        for h in range(chunks):
            copies[p, h].wait_recv()
            pass_on(p, h)

    for h in range(chunks):
        span = slice(h * width, (h + 1) * width)
        hour, cols = h // splits, place(h)[1]
        total = all_ref[h, 0]
        for p in range(1, n):
            total = total + all_ref[h, p]
        mean = jnp.sum(total, 0, keepdims=True) / members
        over = math.sqrt(members - 1.0) * spread[hour : hour + 1, cols]
        for p in range(n):
            scaled = (all_ref[h, p] - mean) / over
            high = scaled.astype(jnp.bfloat16)
            high_ref[p * rows : (p + 1) * rows, span] = high
            low_ref[p * rows : (p + 1) * rows, span] = (
                scaled - high.astype(jnp.float32)
            ).astype(jnp.bfloat16)

    def product(a, b):
        return lax.dot_general(
            a, b, (((1,), (1,)), ((), ())), preferred_element_type=jnp.float32
        )

    used = members + rows
    part_ref[:used, :] = (
        product(high_ref[...], high_ref[:members, :])
        + product(high_ref[...], low_ref[:members, :])
        + product(low_ref[...], high_ref[:members, :])
    )
    if padded > rows:
        part_ref[used:, :] = jnp.zeros((padded - rows, members), jnp.float32)

    piece_g = members // (2 * n_basin)
    piece_c = padded // n_basin

    def gram_rows(side, which):
        return pl.ds(pl.multiple_of((side * n_basin + which) * piece_g, piece_g), piece_g)

    def cross_rows(which):
        return pl.ds(pl.multiple_of(members + which * piece_c, piece_c), piece_c)

    first = []
    for i in range(1, n_basin):
        peer = lax.rem(basin + i, n_basin)
        for src, dst, out_sem, in_sem in (
            (part_ref.at[gram_rows(0, peer)], land_g.at[i - 1], gram_send, gram_recv),
            (part_ref.at[cross_rows(peer)], land_c.at[i - 1], cross_send, cross_recv),
        ):
            first.append(
                pltpu.make_async_remote_copy(
                    src_ref=src, dst_ref=dst,
                    send_sem=out_sem.at[i - 1], recv_sem=in_sem.at[i - 1],
                    device_id={"basin": peer}, device_id_type=MESH,
                )
            )
    for copy in first:
        copy.start()
    for copy in first:
        copy.wait_recv()
    total_g = part_ref[gram_rows(0, basin), :]
    total_c = part_ref[cross_rows(basin), :]
    for i in range(1, n_basin):
        total_g = total_g + land_g[i - 1]
        total_c = total_c + land_c[i - 1]
    sums_ref[gram_rows(0, basin), :] = total_g
    sums_ref[cross_rows(basin), :] = total_c

    def spread_copy(span, i, out_sem, in_sem):
        return pltpu.make_async_remote_copy(
            src_ref=sums_ref.at[span], dst_ref=sums_ref.at[span],
            send_sem=out_sem.at[i - 1], recv_sem=in_sem.at[i - 1],
            device_id={"basin": lax.rem(basin + i, n_basin)}, device_id_type=MESH,
        )

    half = members // 2

    def side_copies(i):
        which = lax.rem(basin - i + n_basin, n_basin)
        return [
            pltpu.make_async_remote_copy(
                src_ref=sums_ref.at[gram_rows(0, which), a * half : (a + 1) * half],
                dst_ref=sums_ref.at[gram_rows(1, which), (1 - a) * half : (2 - a) * half],
                send_sem=side_out.at[i, a], recv_sem=side_in.at[i, a],
                device_id={"member": partners[-1]}, device_id_type=MESH,
            )
            for a in range(2)
        ]

    second = []
    for i in range(1, n_basin):
        second.append(
            (spread_copy(gram_rows(0, basin), i, gram_out, gram_in),
             spread_copy(cross_rows(basin), i, cross_out, cross_in))
        )
    for pair in second:
        for copy in pair:
            copy.start()
    sides = side_copies(0)
    for copy in sides:
        copy.start()
    for i in range(1, n_basin):
        second[i - 1][0].wait_recv()
        passed = side_copies(i)
        for copy in passed:
            copy.start()
        sides = sides + passed
    for pair in second:
        pair[1].wait_recv()
    for copy in sides:
        copy.wait_recv()
    for copy in list(copies.values()) + first + sides:
        copy.wait_send()
    for h in range(chunks):
        for i in range(1, n_basin):
            @pl.when(basin + i < n_basin)
            def _():
                part_copy(i, h).wait_send()
    for pair in second:
        for copy in pair:
            copy.wait_send()


def assimilate(parts, observed, obs_var, obs_noise, collective_id):
    n = lax.axis_size("member")
    nb = lax.axis_size("basin")
    rows, hours, gauges = obs_noise.shape
    width = hours * gauges
    chunks = 2 * hours if gauges % (2 * LANES) == 0 else hours
    members = n * rows
    padded = rows + -rows % (8 * nb)
    f32, bf16 = jnp.float32, jnp.bfloat16
    dma = pltpu.SemaphoreType.DMA
    return pl.pallas_call(
        functools.partial(assimilate_body, hours, nb, n, padded),
        out_shape=(
            jax.ShapeDtypeStruct((rows, hours, gauges), f32),
            jax.ShapeDtypeStruct((members + padded, members), f32),
        ),
        in_specs=[vmem_spec()] * 4,
        out_specs=(vmem_spec(), vmem_spec()),
        scratch_shapes=[
            VMEM((chunks, n, rows, width // chunks), f32),
            VMEM((nb - 1, chunks, rows, width // chunks), f32),
            VMEM((members + rows, width), bf16),
            VMEM((members + rows, width), bf16),
            VMEM((members + padded, members), f32),
            VMEM((nb - 1, members // (2 * nb), members), f32),
            VMEM((nb - 1, padded // nb, members), f32),
        ]
        + [dma((nb - 1, chunks))] * 2
        + [dma((n - 1, chunks))] * 2
        + [dma((nb - 1,))] * 8
        + [dma((nb, 2))] * 2,
        compiler_params=pltpu.CompilerParams(collective_id=collective_id, has_side_effects=True),
        name=f"assimilate_{collective_id}",
    )(parts, observed, obs_var, obs_noise)


def permuted_step(held, axis, bit):
    n = lax.axis_size(axis)
    other = lax.ppermute(held, axis, [(i, i ^ bit) for i in range(n)])
    return jnp.concatenate([held, other], 0)


def split_two(values):
    high = values.astype(jnp.bfloat16)
    low = (values - high.astype(jnp.float32)).astype(jnp.bfloat16)
    return jnp.concatenate([high, low], axis=1)


def route_body(
    seg_count, level_count, members, gauges, hours, param_count,
    basin_ref, coef_ref, given_ref, prior_ref, cos_ref, pin_ref, pout_ref, lat_hbm,
    out_ref,
    up_ref, flow_ref, row_ref, now_ref, back_ref, carry_ref, par_ref, raw_ref, ready_ref,
    int_ref, table_ref, sem, table_sem,
):
    first = basin_ref[0]
    lev = BLK_LEV
    seg_blocks = level_count * lev
    rows = members
    packs = LANES // members
    shape = (rows, LANES)
    lane = lax.broadcasted_iota(jnp.int32, shape, 1)
    place = (lane // members) * members + lax.broadcasted_iota(jnp.int32, shape, 0)

    chunks = sem.shape[0]
    chunk_rows = seg_blocks * hours // chunks

    def fetch(c, m):
        span = pl.ds(c * chunk_rows, chunk_rows)
        return pltpu.make_async_copy(lat_hbm.at[m, span], raw_ref.at[span, m], sem.at[c, m])

    for c in range(chunks):
        for m in range(members):
            fetch(c, m).start()

    tile = int_ref.shape[1]
    tile_sub = lax.broadcasted_iota(jnp.int32, (tile, LANES), 0)

    def integers(seg, _):
        value = given_ref[seg]
        row = value // LANES * (hours * members) + value % members
        int_ref[seg] = jnp.where(tile_sub < 2, value, row)
        return 0

    lax.fori_loop(first, seg_count, integers, 0)
    table = pltpu.make_async_copy(int_ref, table_ref, table_sem)
    table.start()

    def clear(i, _):
        up_ref[i] = jnp.zeros((2 * rows, LANES), jnp.float32)
        return 0

    lax.fori_loop(lev, 2 * lev, clear, 0, unroll=8)

    def turned(values):
        return jnp.concatenate([values] * packs, axis=0).T

    def coefficients(seg, _):
        storage = 0.02 + 0.1 * jax.nn.sigmoid(coef_ref[seg, :, 0, :])
        weighting = 0.2 * jax.nn.sigmoid(coef_ref[seg, :, 1, :])
        den = storage * (1.0 - weighting) + 0.5
        span = pl.ds(pl.multiple_of(seg * seg_blocks, seg_blocks), seg_blocks)
        now_ref[span, :] = turned((0.5 - storage * weighting) / den)
        back_ref[span, :] = turned((0.5 + storage * weighting) / den)
        carry_ref[span, :] = turned((storage * (1.0 - weighting) - 0.5) / den)
        return 0

    lax.fori_loop(first, seg_count, coefficients, 0)
    for k in range(param_count - 2):
        par_ref[k] = turned(0.2 * prior_ref[:, 2 + k, :])

    group_of = lane // members
    row_group = lax.broadcasted_iota(jnp.int32, (1, LANES), 1) // members

    def pick(pieces, order, where):
        made = pieces[order(0)]
        for q in range(1, packs):
            made = jnp.where(where == q, pieces[order(q)], made)
        return made

    def place_group(tiles, where):
        mixed = [pick(tiles, lambda q, g=g: (g - q) % packs, where) for g in range(packs)]
        mixed = [jnp.broadcast_to(tile, shape) for tile in mixed]
        flat = jnp.concatenate(mixed, axis=0).T
        strips = [flat[q * rows : (q + 1) * rows] for q in range(packs)]
        made = []
        for i in range(packs):
            turn = pick(strips, lambda g, i=i: (g - i) % packs, group_of)
            made.append(pltpu.roll(turn, LANES - i * members, 1) if i else turn)
        return made

    def relayout(group, _):
        base = group * packs
        for h in range(hours):
            tiles = [raw_ref[(base + i) * hours + h] for i in range(packs)]
            for i, tile in enumerate(place_group(tiles, group_of)):
                ready_ref[base + i, h] = tile
        for n, ref in enumerate((pin_ref, pout_ref)):
            tiles = [ref[pl.ds(base + i, 1), :] for i in range(packs)]
            for i, tile in enumerate(place_group(tiles, row_group)):
                ready_ref[base + i, hours + n] = tile
        return 0

    chunk_groups = seg_blocks // packs // chunks
    for c in range(chunks):
        for m in range(members):
            fetch(c, m).wait()
        lax.fori_loop(c * chunk_groups, (c + 1) * chunk_groups, relayout, 0, unroll=4)

    table.wait()

    def sweep(seg, level, parity, own):
        def block(j, _):
            here = level * lev + j
            b = seg * seg_blocks + here
            live = place < table_ref[seg, 1, here]
            now = now_ref[pl.ds(b, 1), :]
            back = back_ref[pl.ds(b, 1), :]
            carry = carry_ref[pl.ds(b, 1), :]
            if own:
                expo = cos_ref[0] * par_ref[0, pl.ds(here, 1), :]
                for k in range(1, cos_ref.shape[0]):
                    expo = expo + cos_ref[k] * par_ref[k, pl.ds(here, 1), :]
                scale = jnp.exp(expo)
                add0 = ready_ref[here, 0] * scale
                add1 = ready_ref[here, 1] * scale
                if level > 0:
                    add0 = add0 + up_ref[parity * lev + j, :rows]
                    add1 = add1 + up_ref[parity * lev + j, rows:]
                in0 = jnp.where(live, add0, 0.0)
                in1 = jnp.where(live, add1, 0.0)
                start = back * ready_ref[here, 2] + carry * ready_ref[here, 3]
                out0 = now * in0 + jnp.where(live, start, 0.0)
            else:
                in0 = jnp.where(live, up_ref[parity * lev + j, :rows], 0.0)
                in1 = jnp.where(live, up_ref[parity * lev + j, rows:], 0.0)
                out0 = now * in0
            out1 = now * in1 + back * in0 + carry * out0
            up_ref[parity * lev + j] = jnp.zeros((2 * rows, LANES), jnp.float32)
            flow_ref[pl.ds(here * 2 * rows, rows), :] = out0
            flow_ref[pl.ds(here * 2 * rows + rows, rows), :] = out1
            target = (1 - parity) * lev + table_ref[seg, 0, here]
            up_ref[target, :rows] += out0
            up_ref[target, rows:] += out1
            return 0

        lax.fori_loop(0, lev, block, 0, unroll=4)

    def observe(seg):
        def part_of(part, _):
            for g in range(LANES):
                row = table_ref[seg, 2 + part, g]
                row_ref[0, g : g + 1, :] = flow_ref[pl.ds(row, 1), :]
                row_ref[1, g : g + 1, :] = flow_ref[pl.ds(row + rows, 1), :]
            slot = given_ref[seg, pl.ds(2 + part, 1), :]
            pack = slot % LANES // members
            span = pl.ds(pl.multiple_of(part * LANES, LANES), LANES)
            for h in range(hours):
                turned_rows = row_ref[h].T
                strips = [turned_rows[q * rows : (q + 1) * rows] for q in range(packs)]
                out_ref[seg, h * members : (h + 1) * members, span] = pick(strips, lambda q: q, pack)
            return 0

        lax.fori_loop(0, gauges // LANES, part_of, 0)

    def nothing(seg, _):
        out_ref[seg] = jnp.zeros(out_ref.shape[1:], jnp.float32)
        return 0

    lax.fori_loop(0, first, nothing, 0)
    for level in range(level_count):
        sweep(first, level, level % 2, True)
    observe(first)

    def later(seg, _):
        for level in range(level_count):
            sweep(seg, level, level % 2, False)
        observe(seg)
        return 0

    lax.fori_loop(first + 1, seg_count, later, 0)


def invert_small(d, panel=8):
    size = d.shape[0]
    lane = lax.broadcasted_iota(jnp.int32, d.shape, 1)
    sub = lax.broadcasted_iota(jnp.int32, d.shape, 0)
    for base in range(0, size, panel):
        cols = [jnp.broadcast_to(d[:, base + i : base + i + 1], d.shape) for i in range(panel)]
        for i in range(panel):
            j = base + i
            pivot = cols[i]
            inv = 1.0 / pivot[j : j + 1, :]
            row = jnp.where(lane[:1] == j, 1.0, d[j : j + 1, :]) * inv
            d = jnp.where(sub == j, row, jnp.where(lane == j, 0.0, d) - pivot * row)
            for l in range(i + 1, panel):
                factor = pivot[base + l : base + l + 1, :] * inv
                cols[l] = jnp.where(sub == j, factor, cols[l] - pivot * factor)
    return d


def exact_dot(a, b):
    return jnp.dot(a, b, precision=exact_mode, preferred_element_type=jnp.float32)


def solve_body(n, size, sums_ref, out_ref, a_ref, l_ref):
    total = n * size
    sub = lax.broadcasted_iota(jnp.int32, (total, total), 0)
    lane = lax.broadcasted_iota(jnp.int32, (total, total), 1)
    a_ref[...] = sums_ref[:total, :] + jnp.where(lane == sub, 1.0, 0.0)
    out_ref[...] = sums_ref[total : total + size, :].T
    for k in range(n):
        span = slice(k * size, (k + 1) * size)
        left = (k * size // LANES) * LANES
        inverse = invert_small(a_ref[span, span])
        right = exact_dot(inverse, out_ref[span, :])
        l_ref[...] = a_ref[:, span]
        l_ref[span, :] = jnp.zeros((size, size), jnp.float32)
        column = l_ref[...]
        if k < n - 1:
            top = exact_dot(inverse, a_ref[span, left:])
            a_ref[:, left:] -= exact_dot(column, top)
            a_ref[span, left:] = top
        out_ref[...] -= exact_dot(column, right)
        out_ref[span, :] = right


def inverse_sinh(values):
    return jnp.log(values + jnp.sqrt(values * values + 1.0))


def shards(
    prior_params, lateral_flow, inflow_start, outflow_start, reach_count, downstream,
    gauge_reach, observed, obs_var, obs_noise,
):
    md, param_count, block_dev = prior_params.shape
    hours = lateral_flow.shape[1]
    gauges = gauge_reach.shape[0]
    basins = lax.axis_size("basin")
    n_member = lax.axis_size("member")
    members = md * n_member
    level_count = block_dev // BLK_LEV
    packs = LANES // md
    f32 = jnp.float32

    prior_steps = doubling_bits(n_member)
    held = permuted_step(prior_params[None], "member", prior_steps[0])

    coef_all, table_all = exchange(
        prior_params, downstream.reshape(1, block_dev), reach_count.reshape(1, block_dev),
        gauge_reach.reshape(-1, block_dev), 1,
    )

    modes = param_count - 2
    lane_pos = np.arange(LANES)
    cosine = np.cos(math.pi * np.arange(modes)[:, None] * (lane_pos[None, :] + 0.5) / LANES)
    cosine = np.swapaxes(cosine.reshape(modes, packs, md), 1, 2)
    cosine = jnp.asarray(np.repeat(cosine, md, axis=2), f32)

    lateral = lateral_flow.reshape(md, hours, block_dev, LANES)
    lateral = jnp.swapaxes(lateral, 1, 2).reshape(md, block_dev * hours, LANES)
    held, coef_all = lax.optimization_barrier((held, coef_all))
    for bit in prior_steps[1:-1]:
        held = permuted_step(held, "member", bit)
    basin_idx = lax.axis_index("basin").astype(jnp.int32).reshape(1)
    seg_coef = VMEM((basins * block_dev, LANES), f32)

    parts = pl.pallas_call(
        functools.partial(route_body, basins, level_count, md, gauges, hours, param_count),
        out_shape=jax.ShapeDtypeStruct((basins, 2 * md, gauges), f32),
        in_specs=[smem_spec()] + [vmem_spec()] * 6 + [pl.BlockSpec(memory_space=pl.ANY)],
        out_specs=vmem_spec(),
        scratch_shapes=[
            VMEM((2 * BLK_LEV, 2 * md, LANES), f32),
            VMEM((block_dev * 2 * md, LANES), f32),
            VMEM((hours, LANES, LANES), f32),
            seg_coef,
            seg_coef,
            seg_coef,
            VMEM((modes, block_dev, LANES), f32),
            VMEM((block_dev * hours, md, LANES), f32),
            VMEM((block_dev, hours + 2, md, LANES), f32),
            VMEM(table_all.shape, jnp.int32),
            SMEM(table_all.shape, jnp.int32),
            pltpu.SemaphoreType.DMA((4, md)),
            pltpu.SemaphoreType.DMA,
        ],
        cost_estimate=pl.CostEstimate(
            flops=40_000_000, bytes_accessed=60_000_000, transcendentals=0
        ),
        name="route",
    )(
        basin_idx, coef_all, table_all, prior_params, cosine,
        inflow_start.reshape(block_dev, LANES), outflow_start.reshape(block_dev, LANES), lateral,
    )
    parts, held = lax.optimization_barrier((parts, held))
    held = permuted_step(held, "member", prior_steps[-1])
    prior_all = held.reshape(members, param_count * block_dev)
    predicted, sums = assimilate(parts, observed, obs_var, obs_noise, 2)
    spread_root = math.sqrt(members - 1.0)
    gain = pl.pallas_call(
        functools.partial(solve_body, n_member, md),
        out_shape=jax.ShapeDtypeStruct((members, md), f32),
        in_specs=[vmem_spec()],
        out_specs=vmem_spec(),
        scratch_shapes=[VMEM((members, members), f32), VMEM((members, md), f32)],
        cost_estimate=pl.CostEstimate(
            flops=40_000_000, bytes_accessed=60_000_000, transcendentals=0
        ),
        name="solve",
    )(sums)

    mean_prior = jnp.sum(prior_all, 0, keepdims=True) / members
    anomaly = (prior_all - mean_prior) / spread_root
    change = lax.dot_general(
        gain, anomaly, (((0,), (0,)), ((), ())), precision=exact_mode, preferred_element_type=f32
    )
    posterior = prior_params + change.reshape(md, param_count, block_dev)
    return (posterior, predicted)


def solution(mesh):
    return jax.shard_map(
        shards,
        mesh=mesh,
        in_specs=(
            P("member", None, "basin"),
            P("member", None, "basin"),
            P("basin"),
            P("basin"),
            P("basin"),
            P("basin"),
            P("basin"),
            P(None, "basin"),
            P(None, "basin"),
            P("member", None, "basin"),
        ),
        out_specs=(P("member", None, "basin"), P("member", None, "basin")),
        check_vma=False,
    )
```

```python
import functools
import math

import jax
import jax.numpy as jnp
from jax import lax
import numpy as np
from jax.experimental import pallas as pl
from jax.experimental.pallas import tpu as pltpu
from jax.sharding import PartitionSpec as P

LANES = 128
BLK_LEV = 64
exact_mode = lax.Precision.HIGHEST
VMEM = pltpu.VMEM
SMEM = pltpu.SMEM
MESH = pl.DeviceIdType.MESH


def vmem_spec():
    return pl.BlockSpec(memory_space=VMEM)


def smem_spec():
    return pl.BlockSpec(memory_space=SMEM)


def exchange_body(
    n, prior_ref, down_ref, count_ref, gauge_ref, coef_ref, table_ref, send_sem, recv_sem, own_sem
):
    me = lax.axis_index("basin")
    barrier = pltpu.get_barrier_semaphore()
    for i in range(1, n):
        @pl.when(me + i < n)
        def _():
            pl.semaphore_signal(
                barrier, inc=1, device_id={"basin": lax.rem(me + i, n)}, device_id_type=MESH
            )
    @pl.when(me > 0)
    def _():
        pl.semaphore_wait(barrier, me)

    gauge_rows = gauge_ref.shape[0]
    pieces = [
        (prior_ref.at[:, 0:2, :], coef_ref.at[me, :, 0:2, :]),
        (down_ref, table_ref.at[me, 0:1, :]),
        (count_ref, table_ref.at[me, 1:2, :]),
        (gauge_ref, table_ref.at[me, 2 : 2 + gauge_rows, :]),
    ]

    def remote(i, k):
        src, dst = pieces[k]
        return pltpu.make_async_remote_copy(
            src_ref=src, dst_ref=dst,
            send_sem=send_sem.at[i - 1, k], recv_sem=recv_sem.at[i - 1, k],
            device_id={"basin": lax.rem(me - i + n, n)}, device_id_type=MESH,
        )

    for i in range(1, n):
        @pl.when(me - i >= 0)
        def _():
            for k in range(len(pieces)):
                remote(i, k).start()
    own = [pltpu.make_async_copy(src, dst, own_sem.at[k]) for k, (src, dst) in enumerate(pieces)]
    for copy in own:
        copy.start()
    for copy in own:
        copy.wait()
    for i in range(1, n):
        @pl.when(me + i < n)
        def _():
            for k in range(len(pieces)):
                remote(i, k).wait_recv()

        @pl.when(me - i >= 0)
        def _():
            for k in range(len(pieces)):
                remote(i, k).wait_send()


def exchange(prior, down, count, gauge, collective_id):
    n = lax.axis_size("basin")
    return pl.pallas_call(
        functools.partial(exchange_body, n),
        out_shape=(
            jax.ShapeDtypeStruct((n,) + prior.shape, prior.dtype),
            jax.ShapeDtypeStruct((n, 8, LANES), down.dtype),
        ),
        in_specs=[vmem_spec()] * 4,
        out_specs=(vmem_spec(), vmem_spec()),
        scratch_shapes=[
            pltpu.SemaphoreType.DMA((n - 1, 4)),
            pltpu.SemaphoreType.DMA((n - 1, 4)),
            pltpu.SemaphoreType.DMA((4,)),
        ],
        compiler_params=pltpu.CompilerParams(collective_id=collective_id, has_side_effects=True),
        name=f"exchange_{collective_id}",
    )(prior, down, count, gauge)


def doubling_bits(n):
    bits = []
    bit = n // 2
    while bit:
        bits.append(bit)
        bit //= 2
    return bits


def assimilate_body(
    hours, n_basin, n, padded,
    x_ref, obs_ref, var_ref, noise_ref, pred_ref, sums_ref,
    all_ref, land_ref, high_ref, low_ref, part_ref, land_g, land_c,
    part_send, part_recv, send_sem, recv_sem,
    gram_send, gram_recv, cross_send, cross_recv,
    gram_out, gram_in, cross_out, cross_in, side_out, side_in,
):
    basin = lax.axis_index("basin")
    me = lax.axis_index("member")
    rows = all_ref.shape[2]
    chunks, width = all_ref.shape[0], all_ref.shape[3]
    splits = chunks // hours
    members = n * rows
    partners = [me + bit * (1 - 2 * lax.rem(me // bit, 2)) for bit in doubling_bits(n)]
    barrier = pltpu.get_barrier_semaphore()
    for i in range(1, n_basin):
        @pl.when(basin - i >= 0)
        def _():
            pl.semaphore_signal(
                barrier, inc=1, device_id={"basin": lax.rem(basin - i + n_basin, n_basin)},
                device_id_type=MESH,
            )
    for partner in partners:
        pl.semaphore_signal(barrier, inc=1, device_id={"member": partner}, device_id_type=MESH)
    pl.semaphore_wait(barrier, n_basin - 1 - basin + len(partners))

    def place(h):
        hour, split = h // splits, h % splits
        return slice(hour * rows, (hour + 1) * rows), slice(split * width, (split + 1) * width)

    def part_copy(i, h):
        peer = lax.rem(basin + i, n_basin)
        return pltpu.make_async_remote_copy(
            src_ref=x_ref.at[(peer,) + place(h)], dst_ref=land_ref.at[i - 1, h],
            send_sem=part_send.at[i - 1, h], recv_sem=part_recv.at[i - 1, h],
            device_id={"basin": peer}, device_id_type=MESH,
        )

    for h in range(chunks):
        for i in range(n_basin - 1, 0, -1):
            @pl.when(basin + i < n_basin)
            def _():
                part_copy(i, h).start()

    copies = {}

    def pass_on(p, h):
        for k, partner in enumerate(partners):
            to = 2**k + p
            if p < 2**k:
                copies[to, h] = pltpu.make_async_remote_copy(
                    src_ref=all_ref.at[h, p], dst_ref=all_ref.at[h, to],
                    send_sem=send_sem.at[to - 1, h], recv_sem=recv_sem.at[to - 1, h],
                    device_id={"member": partner}, device_id_type=MESH,
                )
                copies[to, h].start()

    spread = 2.0 * jnp.sqrt(var_ref[...])
    for h in range(chunks):
        all_ref[h, 0] = x_ref[(basin,) + place(h)]
        for i in range(1, n_basin):
            @pl.when(basin - i >= 0)
            def _():
                part_copy(i, h).wait_recv()
                all_ref[h, 0] += land_ref[i - 1, h]
        all_ref[h, 0] = inverse_sinh(all_ref[h, 0])
        pass_on(0, h)
    for h in range(chunks):
        span = slice(h * width, (h + 1) * width)
        hour, cols = h // splits, place(h)[1]
        wide = spread[hour : hour + 1, cols]
        flow = all_ref[h, 0]
        pred_ref[:, hour, cols] = flow
        away = (obs_ref[hour : hour + 1, cols] + wide * noise_ref[:, hour, cols] - flow) / wide
        high = away.astype(jnp.bfloat16)
        high_ref[members : members + rows, span] = high
        low_ref[members : members + rows, span] = (
            away - high.astype(jnp.float32)
        ).astype(jnp.bfloat16)
    for p in range(1, n):
        for h in range(chunks):
            copies[p, h].wait_recv()
            pass_on(p, h)

    for h in range(chunks):
        span = slice(h * width, (h + 1) * width)
        hour, cols = h // splits, place(h)[1]
        total = all_ref[h, 0]
        for p in range(1, n):
            total = total + all_ref[h, p]
        mean = jnp.sum(total, 0, keepdims=True) / members
        over = math.sqrt(members - 1.0) * spread[hour : hour + 1, cols]
        for p in range(n):
            scaled = (all_ref[h, p] - mean) / over
            high = scaled.astype(jnp.bfloat16)
            high_ref[p * rows : (p + 1) * rows, span] = high
            low_ref[p * rows : (p + 1) * rows, span] = (
                scaled - high.astype(jnp.float32)
            ).astype(jnp.bfloat16)

    def product(a, b):
        return lax.dot_general(
            a, b, (((1,), (1,)), ((), ())), preferred_element_type=jnp.float32
        )

    used = members + rows
    part_ref[:used, :] = (
        product(high_ref[...], high_ref[:members, :])
        + product(high_ref[...], low_ref[:members, :])
        + product(low_ref[...], high_ref[:members, :])
    )
    if padded > rows:
        part_ref[used:, :] = jnp.zeros((padded - rows, members), jnp.float32)

    piece_g = members // (2 * n_basin)
    piece_c = padded // n_basin

    def gram_rows(side, which):
        return pl.ds(pl.multiple_of((side * n_basin + which) * piece_g, piece_g), piece_g)

    def cross_rows(which):
        return pl.ds(pl.multiple_of(members + which * piece_c, piece_c), piece_c)

    first = []
    for i in range(1, n_basin):
        peer = lax.rem(basin + i, n_basin)
        for src, dst, out_sem, in_sem in (
            (part_ref.at[gram_rows(0, peer)], land_g.at[i - 1], gram_send, gram_recv),
            (part_ref.at[cross_rows(peer)], land_c.at[i - 1], cross_send, cross_recv),
        ):
            first.append(
                pltpu.make_async_remote_copy(
                    src_ref=src, dst_ref=dst,
                    send_sem=out_sem.at[i - 1], recv_sem=in_sem.at[i - 1],
                    device_id={"basin": peer}, device_id_type=MESH,
                )
            )
    for copy in first:
        copy.start()
    for copy in first:
        copy.wait_recv()
    total_g = part_ref[gram_rows(0, basin), :]
    total_c = part_ref[cross_rows(basin), :]
    for i in range(1, n_basin):
        total_g = total_g + land_g[i - 1]
        total_c = total_c + land_c[i - 1]
    sums_ref[gram_rows(0, basin), :] = total_g
    sums_ref[cross_rows(basin), :] = total_c

    def spread_copy(span, i, out_sem, in_sem):
        return pltpu.make_async_remote_copy(
            src_ref=sums_ref.at[span], dst_ref=sums_ref.at[span],
            send_sem=out_sem.at[i - 1], recv_sem=in_sem.at[i - 1],
            device_id={"basin": lax.rem(basin + i, n_basin)}, device_id_type=MESH,
        )

    half = members // 2

    def side_copies(i):
        which = lax.rem(basin - i + n_basin, n_basin)
        return [
            pltpu.make_async_remote_copy(
                src_ref=sums_ref.at[gram_rows(0, which), a * half : (a + 1) * half],
                dst_ref=sums_ref.at[gram_rows(1, which), (1 - a) * half : (2 - a) * half],
                send_sem=side_out.at[i, a], recv_sem=side_in.at[i, a],
                device_id={"member": partners[-1]}, device_id_type=MESH,
            )
            for a in range(2)
        ]

    second = []
    for i in range(1, n_basin):
        second.append(
            (spread_copy(gram_rows(0, basin), i, gram_out, gram_in),
             spread_copy(cross_rows(basin), i, cross_out, cross_in))
        )
    for pair in second:
        for copy in pair:
            copy.start()
    sides = side_copies(0)
    for copy in sides:
        copy.start()
    for i in range(1, n_basin):
        second[i - 1][0].wait_recv()
        passed = side_copies(i)
        for copy in passed:
            copy.start()
        sides = sides + passed
    for pair in second:
        pair[1].wait_recv()
    for copy in sides:
        copy.wait_recv()
    for copy in list(copies.values()) + first + sides:
        copy.wait_send()
    for h in range(chunks):
        for i in range(1, n_basin):
            @pl.when(basin + i < n_basin)
            def _():
                part_copy(i, h).wait_send()
    for pair in second:
        for copy in pair:
            copy.wait_send()


def assimilate(parts, observed, obs_var, obs_noise, collective_id):
    n = lax.axis_size("member")
    nb = lax.axis_size("basin")
    rows, hours, gauges = obs_noise.shape
    width = hours * gauges
    chunks = 2 * hours if gauges % (2 * LANES) == 0 else hours
    members = n * rows
    padded = rows + -rows % (8 * nb)
    f32, bf16 = jnp.float32, jnp.bfloat16
    dma = pltpu.SemaphoreType.DMA
    return pl.pallas_call(
        functools.partial(assimilate_body, hours, nb, n, padded),
        out_shape=(
            jax.ShapeDtypeStruct((rows, hours, gauges), f32),
            jax.ShapeDtypeStruct((members + padded, members), f32),
        ),
        in_specs=[vmem_spec()] * 4,
        out_specs=(vmem_spec(), vmem_spec()),
        scratch_shapes=[
            VMEM((chunks, n, rows, width // chunks), f32),
            VMEM((nb - 1, chunks, rows, width // chunks), f32),
            VMEM((members + rows, width), bf16),
            VMEM((members + rows, width), bf16),
            VMEM((members + padded, members), f32),
            VMEM((nb - 1, members // (2 * nb), members), f32),
            VMEM((nb - 1, padded // nb, members), f32),
        ]
        + [dma((nb - 1, chunks))] * 2
        + [dma((n - 1, chunks))] * 2
        + [dma((nb - 1,))] * 8
        + [dma((nb, 2))] * 2,
        compiler_params=pltpu.CompilerParams(collective_id=collective_id, has_side_effects=True),
        name=f"assimilate_{collective_id}",
    )(parts, observed, obs_var, obs_noise)


def permuted_step(held, axis, bit):
    n = lax.axis_size(axis)
    other = lax.ppermute(held, axis, [(i, i ^ bit) for i in range(n)])
    return jnp.concatenate([held, other], 0)


def split_two(values):
    high = values.astype(jnp.bfloat16)
    low = (values - high.astype(jnp.float32)).astype(jnp.bfloat16)
    return jnp.concatenate([high, low], axis=1)


def route_body(
    seg_count, level_count, members, gauges, hours, param_count,
    basin_ref, coef_ref, given_ref, prior_ref, cos_ref, pin_ref, pout_ref, lat_hbm,
    out_ref,
    up_ref, flow_ref, row_ref, now_ref, back_ref, carry_ref, par_ref, raw_ref, ready_ref,
    int_ref, table_ref, sem, table_sem,
):
    first = basin_ref[0]
    lev = BLK_LEV
    seg_blocks = level_count * lev
    rows = members
    packs = LANES // members
    shape = (rows, LANES)
    lane = lax.broadcasted_iota(jnp.int32, shape, 1)
    place = (lane // members) * members + lax.broadcasted_iota(jnp.int32, shape, 0)

    chunks = sem.shape[0]
    chunk_rows = seg_blocks * hours // chunks

    def fetch(c, m):
        span = pl.ds(c * chunk_rows, chunk_rows)
        return pltpu.make_async_copy(lat_hbm.at[m, span], raw_ref.at[span, m], sem.at[c, m])

    for c in range(chunks):
        for m in range(members):
            fetch(c, m).start()

    tile = int_ref.shape[1]
    tile_sub = lax.broadcasted_iota(jnp.int32, (tile, LANES), 0)

    def integers(seg, _):
        value = given_ref[seg]
        row = value // LANES * (hours * members) + value % members
        int_ref[seg] = jnp.where(tile_sub < 2, value, row)
        return 0

    lax.fori_loop(first, seg_count, integers, 0)
    table = pltpu.make_async_copy(int_ref, table_ref, table_sem)
    table.start()

    def clear(i, _):
        up_ref[i] = jnp.zeros((2 * rows, LANES), jnp.float32)
        return 0

    lax.fori_loop(lev, 2 * lev, clear, 0, unroll=8)

    def turned(values):
        return jnp.concatenate([values] * packs, axis=0).T

    def coefficients(seg, _):
        storage = 0.02 + 0.1 * jax.nn.sigmoid(coef_ref[seg, :, 0, :])
        weighting = 0.2 * jax.nn.sigmoid(coef_ref[seg, :, 1, :])
        den = storage * (1.0 - weighting) + 0.5
        span = pl.ds(pl.multiple_of(seg * seg_blocks, seg_blocks), seg_blocks)
        now_ref[span, :] = turned((0.5 - storage * weighting) / den)
        back_ref[span, :] = turned((0.5 + storage * weighting) / den)
        carry_ref[span, :] = turned((storage * (1.0 - weighting) - 0.5) / den)
        return 0

    lax.fori_loop(first, seg_count, coefficients, 0)
    for k in range(param_count - 2):
        par_ref[k] = turned(0.2 * prior_ref[:, 2 + k, :])

    group_of = lane // members
    row_group = lax.broadcasted_iota(jnp.int32, (1, LANES), 1) // members

    def pick(pieces, order, where):
        made = pieces[order(0)]
        for q in range(1, packs):
            made = jnp.where(where == q, pieces[order(q)], made)
        return made

    def place_group(tiles, where):
        mixed = [pick(tiles, lambda q, g=g: (g - q) % packs, where) for g in range(packs)]
        mixed = [jnp.broadcast_to(tile, shape) for tile in mixed]
        flat = jnp.concatenate(mixed, axis=0).T
        strips = [flat[q * rows : (q + 1) * rows] for q in range(packs)]
        made = []
        for i in range(packs):
            turn = pick(strips, lambda g, i=i: (g - i) % packs, group_of)
            made.append(pltpu.roll(turn, LANES - i * members, 1) if i else turn)
        return made

    def relayout(group, _):
        base = group * packs
        for h in range(hours):
            tiles = [raw_ref[(base + i) * hours + h] for i in range(packs)]
            for i, tile in enumerate(place_group(tiles, group_of)):
                ready_ref[base + i, h] = tile
        for n, ref in enumerate((pin_ref, pout_ref)):
            tiles = [ref[pl.ds(base + i, 1), :] for i in range(packs)]
            for i, tile in enumerate(place_group(tiles, row_group)):
                ready_ref[base + i, hours + n] = tile
        return 0

    chunk_groups = seg_blocks // packs // chunks
    for c in range(chunks):
        for m in range(members):
            fetch(c, m).wait()
        lax.fori_loop(c * chunk_groups, (c + 1) * chunk_groups, relayout, 0, unroll=4)

    table.wait()

    def sweep(seg, level, parity, own):
        def block(j, _):
            here = level * lev + j
            b = seg * seg_blocks + here
            live = place < table_ref[seg, 1, here]
            now = now_ref[pl.ds(b, 1), :]
            back = back_ref[pl.ds(b, 1), :]
            carry = carry_ref[pl.ds(b, 1), :]
            if own:
                expo = cos_ref[0] * par_ref[0, pl.ds(here, 1), :]
                for k in range(1, cos_ref.shape[0]):
                    expo = expo + cos_ref[k] * par_ref[k, pl.ds(here, 1), :]
                scale = jnp.exp(expo)
                add0 = ready_ref[here, 0] * scale
                add1 = ready_ref[here, 1] * scale
                if level > 0:
                    add0 = add0 + up_ref[parity * lev + j, :rows]
                    add1 = add1 + up_ref[parity * lev + j, rows:]
                in0 = jnp.where(live, add0, 0.0)
                in1 = jnp.where(live, add1, 0.0)
                start = back * ready_ref[here, 2] + carry * ready_ref[here, 3]
                out0 = now * in0 + jnp.where(live, start, 0.0)
            else:
                in0 = jnp.where(live, up_ref[parity * lev + j, :rows], 0.0)
                in1 = jnp.where(live, up_ref[parity * lev + j, rows:], 0.0)
                out0 = now * in0
            out1 = now * in1 + back * in0 + carry * out0
            up_ref[parity * lev + j] = jnp.zeros((2 * rows, LANES), jnp.float32)
            flow_ref[pl.ds(here * 2 * rows, rows), :] = out0
            flow_ref[pl.ds(here * 2 * rows + rows, rows), :] = out1
            target = (1 - parity) * lev + table_ref[seg, 0, here]
            up_ref[target, :rows] += out0
            up_ref[target, rows:] += out1
            return 0

        lax.fori_loop(0, lev, block, 0, unroll=4)

    def observe(seg):
        def part_of(part, _):
            for g in range(LANES):
                row = table_ref[seg, 2 + part, g]
                row_ref[0, g : g + 1, :] = flow_ref[pl.ds(row, 1), :]
                row_ref[1, g : g + 1, :] = flow_ref[pl.ds(row + rows, 1), :]
            slot = given_ref[seg, pl.ds(2 + part, 1), :]
            pack = slot % LANES // members
            span = pl.ds(pl.multiple_of(part * LANES, LANES), LANES)
            for h in range(hours):
                turned_rows = row_ref[h].T
                strips = [turned_rows[q * rows : (q + 1) * rows] for q in range(packs)]
                out_ref[seg, h * members : (h + 1) * members, span] = pick(strips, lambda q: q, pack)
            return 0

        lax.fori_loop(0, gauges // LANES, part_of, 0)

    def nothing(seg, _):
        out_ref[seg] = jnp.zeros(out_ref.shape[1:], jnp.float32)
        return 0

    lax.fori_loop(0, first, nothing, 0)
    for level in range(level_count):
        sweep(first, level, level % 2, True)
    observe(first)

    def later(seg, _):
        for level in range(level_count):
            sweep(seg, level, level % 2, False)
        observe(seg)
        return 0

    lax.fori_loop(first + 1, seg_count, later, 0)


def invert_small(d, panel=8):
    size = d.shape[0]
    lane = lax.broadcasted_iota(jnp.int32, d.shape, 1)
    sub = lax.broadcasted_iota(jnp.int32, d.shape, 0)
    for base in range(0, size, panel):
        cols = [jnp.broadcast_to(d[:, base + i : base + i + 1], d.shape) for i in range(panel)]
        for i in range(panel):
            j = base + i
            pivot = cols[i]
            inv = 1.0 / pivot[j : j + 1, :]
            row = jnp.where(lane[:1] == j, 1.0, d[j : j + 1, :]) * inv
            d = jnp.where(sub == j, row, jnp.where(lane == j, 0.0, d) - pivot * row)
            for l in range(i + 1, panel):
                factor = pivot[base + l : base + l + 1, :] * inv
                cols[l] = jnp.where(sub == j, factor, cols[l] - pivot * factor)
    return d


def exact_dot(a, b):
    return jnp.dot(a, b, precision=exact_mode, preferred_element_type=jnp.float32)


def solve_body(n, size, sums_ref, out_ref, a_ref, l_ref):
    total = n * size
    sub = lax.broadcasted_iota(jnp.int32, (total, total), 0)
    lane = lax.broadcasted_iota(jnp.int32, (total, total), 1)
    a_ref[...] = sums_ref[:total, :] + jnp.where(lane == sub, 1.0, 0.0)
    out_ref[...] = sums_ref[total : total + size, :].T
    for k in range(n):
        span = slice(k * size, (k + 1) * size)
        left = (k * size // LANES) * LANES
        inverse = invert_small(a_ref[span, span])
        right = exact_dot(inverse, out_ref[span, :])
        l_ref[...] = a_ref[:, span]
        l_ref[span, :] = jnp.zeros((size, size), jnp.float32)
        column = l_ref[...]
        if k < n - 1:
            top = exact_dot(inverse, a_ref[span, left:])
            a_ref[:, left:] -= exact_dot(column, top)
            a_ref[span, left:] = top
        out_ref[...] -= exact_dot(column, right)
        out_ref[span, :] = right


def inverse_sinh(values):
    return jnp.log(values + jnp.sqrt(values * values + 1.0))


def shards(
    prior_params, lateral_flow, inflow_start, outflow_start, reach_count, downstream,
    gauge_reach, observed, obs_var, obs_noise,
):
    md, param_count, block_dev = prior_params.shape
    hours = lateral_flow.shape[1]
    gauges = gauge_reach.shape[0]
    basins = lax.axis_size("basin")
    n_member = lax.axis_size("member")
    members = md * n_member
    level_count = block_dev // BLK_LEV
    packs = LANES // md
    f32 = jnp.float32

    prior_steps = doubling_bits(n_member)
    held = permuted_step(prior_params[None], "member", prior_steps[0])

    coef_all, table_all = exchange(
        prior_params, downstream.reshape(1, block_dev), reach_count.reshape(1, block_dev),
        gauge_reach.reshape(-1, block_dev), 1,
    )

    modes = param_count - 2
    lane_pos = np.arange(LANES)
    cosine = np.cos(math.pi * np.arange(modes)[:, None] * (lane_pos[None, :] + 0.5) / LANES)
    cosine = np.swapaxes(cosine.reshape(modes, packs, md), 1, 2)
    cosine = jnp.asarray(np.repeat(cosine, md, axis=2), f32)

    lateral = lateral_flow.reshape(md, hours, block_dev, LANES)
    lateral = jnp.swapaxes(lateral, 1, 2).reshape(md, block_dev * hours, LANES)
    held, coef_all = lax.optimization_barrier((held, coef_all))
    for bit in prior_steps[1:-1]:
        held = permuted_step(held, "member", bit)
    basin_idx = lax.axis_index("basin").astype(jnp.int32).reshape(1)
    seg_coef = VMEM((basins * block_dev, LANES), f32)

    parts = pl.pallas_call(
        functools.partial(route_body, basins, level_count, md, gauges, hours, param_count),
        out_shape=jax.ShapeDtypeStruct((basins, 2 * md, gauges), f32),
        in_specs=[smem_spec()] + [vmem_spec()] * 6 + [pl.BlockSpec(memory_space=pl.ANY)],
        out_specs=vmem_spec(),
        scratch_shapes=[
            VMEM((2 * BLK_LEV, 2 * md, LANES), f32),
            VMEM((block_dev * 2 * md, LANES), f32),
            VMEM((hours, LANES, LANES), f32),
            seg_coef,
            seg_coef,
            seg_coef,
            VMEM((modes, block_dev, LANES), f32),
            VMEM((block_dev * hours, md, LANES), f32),
            VMEM((block_dev, hours + 2, md, LANES), f32),
            VMEM(table_all.shape, jnp.int32),
            SMEM(table_all.shape, jnp.int32),
            pltpu.SemaphoreType.DMA((8, md)),
            pltpu.SemaphoreType.DMA,
        ],
        cost_estimate=pl.CostEstimate(
            flops=40_000_000, bytes_accessed=60_000_000, transcendentals=0
        ),
        name="route",
    )(
        basin_idx, coef_all, table_all, prior_params, cosine,
        inflow_start.reshape(block_dev, LANES), outflow_start.reshape(block_dev, LANES), lateral,
    )
    parts, held = lax.optimization_barrier((parts, held))
    held = permuted_step(held, "member", prior_steps[-1])
    prior_all = held.reshape(members, param_count * block_dev)
    predicted, sums = assimilate(parts, observed, obs_var, obs_noise, 2)
    spread_root = math.sqrt(members - 1.0)
    gain = pl.pallas_call(
        functools.partial(solve_body, n_member, md),
        out_shape=jax.ShapeDtypeStruct((members, md), f32),
        in_specs=[vmem_spec()],
        out_specs=vmem_spec(),
        scratch_shapes=[VMEM((members, members), f32), VMEM((members, md), f32)],
        cost_estimate=pl.CostEstimate(
            flops=40_000_000, bytes_accessed=60_000_000, transcendentals=0
        ),
        name="solve",
    )(sums)

    mean_prior = jnp.sum(prior_all, 0, keepdims=True) / members
    anomaly = (prior_all - mean_prior) / spread_root
    change = lax.dot_general(
        gain, anomaly, (((0,), (0,)), ((), ())), precision=exact_mode, preferred_element_type=f32
    )
    posterior = prior_params + change.reshape(md, param_count, block_dev)
    return (posterior, predicted)


def solution(mesh):
    return jax.shard_map(
        shards,
        mesh=mesh,
        in_specs=(
            P("member", None, "basin"),
            P("member", None, "basin"),
            P("basin"),
            P("basin"),
            P("basin"),
            P("basin"),
            P("basin"),
            P(None, "basin"),
            P(None, "basin"),
            P("member", None, "basin"),
        ),
        out_specs=(P("member", None, "basin"), P("member", None, "basin")),
        check_vma=False,
    )
```

```python
import functools
import math

import jax
import jax.numpy as jnp
from jax import lax
import numpy as np
from jax.experimental import pallas as pl
from jax.experimental.pallas import tpu as pltpu
from jax.sharding import PartitionSpec as P

LANES = 128
BLK_LEV = 64
exact_mode = lax.Precision.HIGHEST
VMEM = pltpu.VMEM
SMEM = pltpu.SMEM
MESH = pl.DeviceIdType.MESH


def vmem_spec():
    return pl.BlockSpec(memory_space=VMEM)


def smem_spec():
    return pl.BlockSpec(memory_space=SMEM)


def exchange_body(
    n, prior_ref, down_ref, count_ref, gauge_ref, coef_ref, table_ref, send_sem, recv_sem, own_sem
):
    me = lax.axis_index("basin")
    barrier = pltpu.get_barrier_semaphore()
    for i in range(1, n):
        @pl.when(me + i < n)
        def _():
            pl.semaphore_signal(
                barrier, inc=1, device_id={"basin": lax.rem(me + i, n)}, device_id_type=MESH
            )
    @pl.when(me > 0)
    def _():
        pl.semaphore_wait(barrier, me)

    gauge_rows = gauge_ref.shape[0]
    pieces = [
        (prior_ref.at[:, 0:2, :], coef_ref.at[me, :, 0:2, :]),
        (down_ref, table_ref.at[me, 0:1, :]),
        (count_ref, table_ref.at[me, 1:2, :]),
        (gauge_ref, table_ref.at[me, 2 : 2 + gauge_rows, :]),
    ]

    def remote(i, k):
        src, dst = pieces[k]
        return pltpu.make_async_remote_copy(
            src_ref=src, dst_ref=dst,
            send_sem=send_sem.at[i - 1, k], recv_sem=recv_sem.at[i - 1, k],
            device_id={"basin": lax.rem(me - i + n, n)}, device_id_type=MESH,
        )

    for i in range(1, n):
        @pl.when(me - i >= 0)
        def _():
            for k in range(len(pieces)):
                remote(i, k).start()
    own = [pltpu.make_async_copy(src, dst, own_sem.at[k]) for k, (src, dst) in enumerate(pieces)]
    for copy in own:
        copy.start()
    for copy in own:
        copy.wait()
    for i in range(1, n):
        @pl.when(me + i < n)
        def _():
            for k in range(len(pieces)):
                remote(i, k).wait_recv()

        @pl.when(me - i >= 0)
        def _():
            for k in range(len(pieces)):
                remote(i, k).wait_send()


def exchange(prior, down, count, gauge, collective_id):
    n = lax.axis_size("basin")
    return pl.pallas_call(
        functools.partial(exchange_body, n),
        out_shape=(
            jax.ShapeDtypeStruct((n,) + prior.shape, prior.dtype),
            jax.ShapeDtypeStruct((n, 8, LANES), down.dtype),
        ),
        in_specs=[vmem_spec()] * 4,
        out_specs=(vmem_spec(), vmem_spec()),
        scratch_shapes=[
            pltpu.SemaphoreType.DMA((n - 1, 4)),
            pltpu.SemaphoreType.DMA((n - 1, 4)),
            pltpu.SemaphoreType.DMA((4,)),
        ],
        compiler_params=pltpu.CompilerParams(collective_id=collective_id, has_side_effects=True),
        name=f"exchange_{collective_id}",
    )(prior, down, count, gauge)


def doubling_bits(n):
    bits = []
    bit = n // 2
    while bit:
        bits.append(bit)
        bit //= 2
    return bits


def assimilate_body(
    hours, n_basin, n, padded,
    x_ref, obs_ref, var_ref, noise_ref, pred_ref, sums_ref,
    all_ref, land_ref, high_ref, low_ref, part_ref, land_g, land_c,
    part_send, part_recv, send_sem, recv_sem,
    gram_send, gram_recv, cross_send, cross_recv,
    gram_out, gram_in, cross_out, cross_in, side_out, side_in,
):
    basin = lax.axis_index("basin")
    me = lax.axis_index("member")
    rows = all_ref.shape[2]
    chunks, width = all_ref.shape[0], all_ref.shape[3]
    splits = chunks // hours
    members = n * rows
    partners = [me + bit * (1 - 2 * lax.rem(me // bit, 2)) for bit in doubling_bits(n)]
    barrier = pltpu.get_barrier_semaphore()
    for i in range(1, n_basin):
        @pl.when(basin - i >= 0)
        def _():
            pl.semaphore_signal(
                barrier, inc=1, device_id={"basin": lax.rem(basin - i + n_basin, n_basin)},
                device_id_type=MESH,
            )
    for partner in partners:
        pl.semaphore_signal(barrier, inc=1, device_id={"member": partner}, device_id_type=MESH)
    pl.semaphore_wait(barrier, n_basin - 1 - basin + len(partners))

    def place(h):
        hour, split = h // splits, h % splits
        return slice(hour * rows, (hour + 1) * rows), slice(split * width, (split + 1) * width)

    def part_copy(i, h):
        peer = lax.rem(basin + i, n_basin)
        return pltpu.make_async_remote_copy(
            src_ref=x_ref.at[(peer,) + place(h)], dst_ref=land_ref.at[i - 1, h],
            send_sem=part_send.at[i - 1, h], recv_sem=part_recv.at[i - 1, h],
            device_id={"basin": peer}, device_id_type=MESH,
        )

    for h in range(chunks):
        for i in range(n_basin - 1, 0, -1):
            @pl.when(basin + i < n_basin)
            def _():
                part_copy(i, h).start()

    copies = {}

    def pass_on(p, h):
        for k, partner in enumerate(partners):
            to = 2**k + p
            if p < 2**k:
                copies[to, h] = pltpu.make_async_remote_copy(
                    src_ref=all_ref.at[h, p], dst_ref=all_ref.at[h, to],
                    send_sem=send_sem.at[to - 1, h], recv_sem=recv_sem.at[to - 1, h],
                    device_id={"member": partner}, device_id_type=MESH,
                )
                copies[to, h].start()

    spread = 2.0 * jnp.sqrt(var_ref[...])
    for h in range(chunks):
        all_ref[h, 0] = x_ref[(basin,) + place(h)]
        for i in range(1, n_basin):
            @pl.when(basin - i >= 0)
            def _():
                part_copy(i, h).wait_recv()
                all_ref[h, 0] += land_ref[i - 1, h]
        all_ref[h, 0] = inverse_sinh(all_ref[h, 0])
        pass_on(0, h)
    for h in range(chunks):
        span = slice(h * width, (h + 1) * width)
        hour, cols = h // splits, place(h)[1]
        wide = spread[hour : hour + 1, cols]
        flow = all_ref[h, 0]
        pred_ref[:, hour, cols] = flow
        away = (obs_ref[hour : hour + 1, cols] + wide * noise_ref[:, hour, cols] - flow) / wide
        high = away.astype(jnp.bfloat16)
        high_ref[members : members + rows, span] = high
        low_ref[members : members + rows, span] = (
            away - high.astype(jnp.float32)
        ).astype(jnp.bfloat16)
    for p in range(1, n):
        for h in range(chunks):
            copies[p, h].wait_recv()
            pass_on(p, h)

    for h in range(chunks):
        span = slice(h * width, (h + 1) * width)
        hour, cols = h // splits, place(h)[1]
        total = all_ref[h, 0]
        for p in range(1, n):
            total = total + all_ref[h, p]
        mean = jnp.sum(total, 0, keepdims=True) / members
        over = math.sqrt(members - 1.0) * spread[hour : hour + 1, cols]
        for p in range(n):
            scaled = (all_ref[h, p] - mean) / over
            high = scaled.astype(jnp.bfloat16)
            high_ref[p * rows : (p + 1) * rows, span] = high
            low_ref[p * rows : (p + 1) * rows, span] = (
                scaled - high.astype(jnp.float32)
            ).astype(jnp.bfloat16)

    def product(a, b):
        return lax.dot_general(
            a, b, (((1,), (1,)), ((), ())), preferred_element_type=jnp.float32
        )

    used = members + rows
    part_ref[:used, :] = (
        product(high_ref[...], high_ref[:members, :])
        + product(high_ref[...], low_ref[:members, :])
        + product(low_ref[...], high_ref[:members, :])
    )
    if padded > rows:
        part_ref[used:, :] = jnp.zeros((padded - rows, members), jnp.float32)

    piece_g = members // (2 * n_basin)
    piece_c = padded // n_basin

    def gram_rows(side, which):
        return pl.ds(pl.multiple_of((side * n_basin + which) * piece_g, piece_g), piece_g)

    def cross_rows(which):
        return pl.ds(pl.multiple_of(members + which * piece_c, piece_c), piece_c)

    first = []
    for i in range(1, n_basin):
        peer = lax.rem(basin + i, n_basin)
        for src, dst, out_sem, in_sem in (
            (part_ref.at[gram_rows(0, peer)], land_g.at[i - 1], gram_send, gram_recv),
            (part_ref.at[cross_rows(peer)], land_c.at[i - 1], cross_send, cross_recv),
        ):
            first.append(
                pltpu.make_async_remote_copy(
                    src_ref=src, dst_ref=dst,
                    send_sem=out_sem.at[i - 1], recv_sem=in_sem.at[i - 1],
                    device_id={"basin": peer}, device_id_type=MESH,
                )
            )
    for copy in first:
        copy.start()
    for copy in first:
        copy.wait_recv()
    total_g = part_ref[gram_rows(0, basin), :]
    total_c = part_ref[cross_rows(basin), :]
    for i in range(1, n_basin):
        total_g = total_g + land_g[i - 1]
        total_c = total_c + land_c[i - 1]
    sums_ref[gram_rows(0, basin), :] = total_g
    sums_ref[cross_rows(basin), :] = total_c

    def spread_copy(span, i, out_sem, in_sem):
        return pltpu.make_async_remote_copy(
            src_ref=sums_ref.at[span], dst_ref=sums_ref.at[span],
            send_sem=out_sem.at[i - 1], recv_sem=in_sem.at[i - 1],
            device_id={"basin": lax.rem(basin + i, n_basin)}, device_id_type=MESH,
        )

    half = members // 2

    def side_copies(i):
        which = lax.rem(basin - i + n_basin, n_basin)
        return [
            pltpu.make_async_remote_copy(
                src_ref=sums_ref.at[gram_rows(0, which), a * half : (a + 1) * half],
                dst_ref=sums_ref.at[gram_rows(1, which), (1 - a) * half : (2 - a) * half],
                send_sem=side_out.at[i, a], recv_sem=side_in.at[i, a],
                device_id={"member": partners[-1]}, device_id_type=MESH,
            )
            for a in range(2)
        ]

    second = []
    for i in range(1, n_basin):
        second.append(
            (spread_copy(gram_rows(0, basin), i, gram_out, gram_in),
             spread_copy(cross_rows(basin), i, cross_out, cross_in))
        )
    for pair in second:
        for copy in pair:
            copy.start()
    sides = side_copies(0)
    for copy in sides:
        copy.start()
    for i in range(1, n_basin):
        second[i - 1][0].wait_recv()
        passed = side_copies(i)
        for copy in passed:
            copy.start()
        sides = sides + passed
    for pair in second:
        pair[1].wait_recv()
    for copy in sides:
        copy.wait_recv()
    for copy in list(copies.values()) + first + sides:
        copy.wait_send()
    for h in range(chunks):
        for i in range(1, n_basin):
            @pl.when(basin + i < n_basin)
            def _():
                part_copy(i, h).wait_send()
    for pair in second:
        for copy in pair:
            copy.wait_send()


def assimilate(parts, observed, obs_var, obs_noise, collective_id):
    n = lax.axis_size("member")
    nb = lax.axis_size("basin")
    rows, hours, gauges = obs_noise.shape
    width = hours * gauges
    chunks = 2 * hours if gauges % (2 * LANES) == 0 else hours
    members = n * rows
    padded = rows + -rows % (8 * nb)
    f32, bf16 = jnp.float32, jnp.bfloat16
    dma = pltpu.SemaphoreType.DMA
    return pl.pallas_call(
        functools.partial(assimilate_body, hours, nb, n, padded),
        out_shape=(
            jax.ShapeDtypeStruct((rows, hours, gauges), f32),
            jax.ShapeDtypeStruct((members + padded, members), f32),
        ),
        in_specs=[vmem_spec()] * 4,
        out_specs=(vmem_spec(), vmem_spec()),
        scratch_shapes=[
            VMEM((chunks, n, rows, width // chunks), f32),
            VMEM((nb - 1, chunks, rows, width // chunks), f32),
            VMEM((members + rows, width), bf16),
            VMEM((members + rows, width), bf16),
            VMEM((members + padded, members), f32),
            VMEM((nb - 1, members // (2 * nb), members), f32),
            VMEM((nb - 1, padded // nb, members), f32),
        ]
        + [dma((nb - 1, chunks))] * 2
        + [dma((n - 1, chunks))] * 2
        + [dma((nb - 1,))] * 8
        + [dma((nb, 2))] * 2,
        compiler_params=pltpu.CompilerParams(collective_id=collective_id, has_side_effects=True),
        name=f"assimilate_{collective_id}",
    )(parts, observed, obs_var, obs_noise)


def permuted_step(held, axis, bit):
    n = lax.axis_size(axis)
    other = lax.ppermute(held, axis, [(i, i ^ bit) for i in range(n)])
    return jnp.concatenate([held, other], 0)


def split_two(values):
    high = values.astype(jnp.bfloat16)
    low = (values - high.astype(jnp.float32)).astype(jnp.bfloat16)
    return jnp.concatenate([high, low], axis=1)


def route_body(
    seg_count, level_count, members, gauges, hours, param_count,
    basin_ref, coef_ref, given_ref, prior_ref, cos_ref, pin_ref, pout_ref, lat_hbm,
    out_ref,
    up_ref, flow_ref, row_ref, now_ref, back_ref, carry_ref, par_ref, raw_ref, ready_ref,
    int_ref, table_ref, sem, table_sem,
):
    first = basin_ref[0]
    lev = BLK_LEV
    seg_blocks = level_count * lev
    rows = members
    packs = LANES // members
    shape = (rows, LANES)
    lane = lax.broadcasted_iota(jnp.int32, shape, 1)
    place = (lane // members) * members + lax.broadcasted_iota(jnp.int32, shape, 0)

    chunks = sem.shape[0]
    chunk_rows = seg_blocks * hours // chunks

    def fetch(c, m):
        span = pl.ds(c * chunk_rows, chunk_rows)
        return pltpu.make_async_copy(lat_hbm.at[m, span], raw_ref.at[span, m], sem.at[c, m])

    for c in range(chunks):
        for m in range(members):
            fetch(c, m).start()

    tile = int_ref.shape[1]
    tile_sub = lax.broadcasted_iota(jnp.int32, (tile, LANES), 0)

    def integers(seg, _):
        value = given_ref[seg]
        row = value // LANES * (hours * members) + value % members
        int_ref[seg] = jnp.where(tile_sub < 2, value, row)
        return 0

    lax.fori_loop(first, seg_count, integers, 0)
    table = pltpu.make_async_copy(int_ref, table_ref, table_sem)
    table.start()

    def clear(i, _):
        up_ref[i] = jnp.zeros((2 * rows, LANES), jnp.float32)
        return 0

    lax.fori_loop(lev, 2 * lev, clear, 0, unroll=8)

    def turned(values):
        return jnp.concatenate([values] * packs, axis=0).T

    def coefficients(seg, _):
        storage = 0.02 + 0.1 * jax.nn.sigmoid(coef_ref[seg, :, 0, :])
        weighting = 0.2 * jax.nn.sigmoid(coef_ref[seg, :, 1, :])
        den = storage * (1.0 - weighting) + 0.5
        span = pl.ds(pl.multiple_of(seg * seg_blocks, seg_blocks), seg_blocks)
        now_ref[span, :] = turned((0.5 - storage * weighting) / den)
        back_ref[span, :] = turned((0.5 + storage * weighting) / den)
        carry_ref[span, :] = turned((storage * (1.0 - weighting) - 0.5) / den)
        return 0

    lax.fori_loop(first, seg_count, coefficients, 0)
    for k in range(param_count - 2):
        par_ref[k] = turned(0.2 * prior_ref[:, 2 + k, :])

    group_of = lane // members
    row_group = lax.broadcasted_iota(jnp.int32, (1, LANES), 1) // members

    def pick(pieces, order, where):
        made = pieces[order(0)]
        for q in range(1, packs):
            made = jnp.where(where == q, pieces[order(q)], made)
        return made

    def place_group(tiles, where):
        mixed = [pick(tiles, lambda q, g=g: (g - q) % packs, where) for g in range(packs)]
        mixed = [jnp.broadcast_to(tile, shape) for tile in mixed]
        flat = jnp.concatenate(mixed, axis=0).T
        strips = [flat[q * rows : (q + 1) * rows] for q in range(packs)]
        made = []
        for i in range(packs):
            turn = pick(strips, lambda g, i=i: (g - i) % packs, group_of)
            made.append(pltpu.roll(turn, LANES - i * members, 1) if i else turn)
        return made

    def relayout(group, _):
        base = group * packs
        for h in range(hours):
            tiles = [raw_ref[(base + i) * hours + h] for i in range(packs)]
            for i, tile in enumerate(place_group(tiles, group_of)):
                ready_ref[base + i, h] = tile
        for n, ref in enumerate((pin_ref, pout_ref)):
            tiles = [ref[pl.ds(base + i, 1), :] for i in range(packs)]
            for i, tile in enumerate(place_group(tiles, row_group)):
                ready_ref[base + i, hours + n] = tile
        return 0

    chunk_groups = seg_blocks // packs // chunks
    for c in range(chunks):
        for m in range(members):
            fetch(c, m).wait()
        lax.fori_loop(c * chunk_groups, (c + 1) * chunk_groups, relayout, 0, unroll=4)

    table.wait()

    def sweep(seg, level, parity, own):
        def block(j, _):
            here = level * lev + j
            b = seg * seg_blocks + here
            live = place < table_ref[seg, 1, here]
            now = now_ref[pl.ds(b, 1), :]
            back = back_ref[pl.ds(b, 1), :]
            carry = carry_ref[pl.ds(b, 1), :]
            if own:
                expo = cos_ref[0] * par_ref[0, pl.ds(here, 1), :]
                for k in range(1, cos_ref.shape[0]):
                    expo = expo + cos_ref[k] * par_ref[k, pl.ds(here, 1), :]
                scale = jnp.exp(expo)
                add0 = ready_ref[here, 0] * scale
                add1 = ready_ref[here, 1] * scale
                if level > 0:
                    add0 = add0 + up_ref[parity * lev + j, :rows]
                    add1 = add1 + up_ref[parity * lev + j, rows:]
                in0 = jnp.where(live, add0, 0.0)
                in1 = jnp.where(live, add1, 0.0)
                start = back * ready_ref[here, 2] + carry * ready_ref[here, 3]
                out0 = now * in0 + jnp.where(live, start, 0.0)
            else:
                in0 = jnp.where(live, up_ref[parity * lev + j, :rows], 0.0)
                in1 = jnp.where(live, up_ref[parity * lev + j, rows:], 0.0)
                out0 = now * in0
            out1 = now * in1 + back * in0 + carry * out0
            up_ref[parity * lev + j] = jnp.zeros((2 * rows, LANES), jnp.float32)
            flow_ref[pl.ds(here * 2 * rows, rows), :] = out0
            flow_ref[pl.ds(here * 2 * rows + rows, rows), :] = out1
            target = (1 - parity) * lev + table_ref[seg, 0, here]
            up_ref[target, :rows] += out0
            up_ref[target, rows:] += out1
            return 0

        lax.fori_loop(0, lev, block, 0, unroll=4)

    def observe(seg):
        def part_of(part, _):
            for g in range(LANES):
                row = table_ref[seg, 2 + part, g]
                row_ref[0, g : g + 1, :] = flow_ref[pl.ds(row, 1), :]
                row_ref[1, g : g + 1, :] = flow_ref[pl.ds(row + rows, 1), :]
            slot = given_ref[seg, pl.ds(2 + part, 1), :]
            pack = slot % LANES // members
            span = pl.ds(pl.multiple_of(part * LANES, LANES), LANES)
            for h in range(hours):
                turned_rows = row_ref[h].T
                strips = [turned_rows[q * rows : (q + 1) * rows] for q in range(packs)]
                out_ref[seg, h * members : (h + 1) * members, span] = pick(strips, lambda q: q, pack)
            return 0

        lax.fori_loop(0, gauges // LANES, part_of, 0)

    def nothing(seg, _):
        out_ref[seg] = jnp.zeros(out_ref.shape[1:], jnp.float32)
        return 0

    lax.fori_loop(0, first, nothing, 0)
    for level in range(level_count):
        sweep(first, level, level % 2, True)
    observe(first)

    def later(seg, _):
        for level in range(level_count):
            sweep(seg, level, level % 2, False)
        observe(seg)
        return 0

    lax.fori_loop(first + 1, seg_count, later, 0)


def invert_small(d, panel=8):
    size = d.shape[0]
    lane = lax.broadcasted_iota(jnp.int32, d.shape, 1)
    sub = lax.broadcasted_iota(jnp.int32, d.shape, 0)
    for base in range(0, size, panel):
        cols = [jnp.broadcast_to(d[:, base + i : base + i + 1], d.shape) for i in range(panel)]
        for i in range(panel):
            j = base + i
            pivot = cols[i]
            inv = 1.0 / pivot[j : j + 1, :]
            row = jnp.where(lane[:1] == j, 1.0, d[j : j + 1, :]) * inv
            d = jnp.where(sub == j, row, jnp.where(lane == j, 0.0, d) - pivot * row)
            for l in range(i + 1, panel):
                factor = pivot[base + l : base + l + 1, :] * inv
                cols[l] = jnp.where(sub == j, factor, cols[l] - pivot * factor)
    return d


def exact_dot(a, b):
    return jnp.dot(a, b, precision=exact_mode, preferred_element_type=jnp.float32)


def solve_body(n, size, sums_ref, out_ref, a_ref, l_ref):
    total = n * size
    sub = lax.broadcasted_iota(jnp.int32, (total, total), 0)
    lane = lax.broadcasted_iota(jnp.int32, (total, total), 1)
    a_ref[...] = sums_ref[:total, :] + jnp.where(lane == sub, 1.0, 0.0)
    out_ref[...] = sums_ref[total : total + size, :].T
    for k in range(n):
        span = slice(k * size, (k + 1) * size)
        left = (k * size // LANES) * LANES
        inverse = invert_small(a_ref[span, span])
        right = exact_dot(inverse, out_ref[span, :])
        l_ref[...] = a_ref[:, span]
        l_ref[span, :] = jnp.zeros((size, size), jnp.float32)
        column = l_ref[...]
        if k < n - 1:
            top = exact_dot(inverse, a_ref[span, left:])
            a_ref[:, left:] -= exact_dot(column, top)
            a_ref[span, left:] = top
        out_ref[...] -= exact_dot(column, right)
        out_ref[span, :] = right


def inverse_sinh(values):
    return jnp.log(values + jnp.sqrt(values * values + 1.0))


def shards(
    prior_params, lateral_flow, inflow_start, outflow_start, reach_count, downstream,
    gauge_reach, observed, obs_var, obs_noise,
):
    md, param_count, block_dev = prior_params.shape
    hours = lateral_flow.shape[1]
    gauges = gauge_reach.shape[0]
    basins = lax.axis_size("basin")
    n_member = lax.axis_size("member")
    members = md * n_member
    level_count = block_dev // BLK_LEV
    packs = LANES // md
    f32 = jnp.float32

    prior_steps = doubling_bits(n_member)
    held = permuted_step(prior_params[None], "member", prior_steps[0])

    coef_all, table_all = exchange(
        prior_params, downstream.reshape(1, block_dev), reach_count.reshape(1, block_dev),
        gauge_reach.reshape(-1, block_dev), 1,
    )

    modes = param_count - 2
    lane_pos = np.arange(LANES)
    cosine = np.cos(math.pi * np.arange(modes)[:, None] * (lane_pos[None, :] + 0.5) / LANES)
    cosine = np.swapaxes(cosine.reshape(modes, packs, md), 1, 2)
    cosine = jnp.asarray(np.repeat(cosine, md, axis=2), f32)

    lateral = lateral_flow.reshape(md, hours, block_dev, LANES)
    lateral = jnp.swapaxes(lateral, 1, 2).reshape(md, block_dev * hours, LANES)
    held, coef_all = lax.optimization_barrier((held, coef_all))
    for bit in prior_steps[1:-1]:
        held = permuted_step(held, "member", bit)
    basin_idx = lax.axis_index("basin").astype(jnp.int32).reshape(1)
    seg_coef = VMEM((basins * block_dev, LANES), f32)

    parts = pl.pallas_call(
        functools.partial(route_body, basins, level_count, md, gauges, hours, param_count),
        out_shape=jax.ShapeDtypeStruct((basins, 2 * md, gauges), f32),
        in_specs=[smem_spec()] + [vmem_spec()] * 6 + [pl.BlockSpec(memory_space=pl.ANY)],
        out_specs=vmem_spec(),
        scratch_shapes=[
            VMEM((2 * BLK_LEV, 2 * md, LANES), f32),
            VMEM((block_dev * 2 * md, LANES), f32),
            VMEM((hours, LANES, LANES), f32),
            seg_coef,
            seg_coef,
            seg_coef,
            VMEM((modes, block_dev, LANES), f32),
            VMEM((block_dev * hours, md, LANES), f32),
            VMEM((block_dev, hours + 2, md, LANES), f32),
            VMEM(table_all.shape, jnp.int32),
            SMEM(table_all.shape, jnp.int32),
            pltpu.SemaphoreType.DMA((2, md)),
            pltpu.SemaphoreType.DMA,
        ],
        cost_estimate=pl.CostEstimate(
            flops=40_000_000, bytes_accessed=60_000_000, transcendentals=0
        ),
        name="route",
    )(
        basin_idx, coef_all, table_all, prior_params, cosine,
        inflow_start.reshape(block_dev, LANES), outflow_start.reshape(block_dev, LANES), lateral,
    )
    parts, held = lax.optimization_barrier((parts, held))
    held = permuted_step(held, "member", prior_steps[-1])
    prior_all = held.reshape(members, param_count * block_dev)
    predicted, sums = assimilate(parts, observed, obs_var, obs_noise, 2)
    spread_root = math.sqrt(members - 1.0)
    gain = pl.pallas_call(
        functools.partial(solve_body, n_member, md),
        out_shape=jax.ShapeDtypeStruct((members, md), f32),
        in_specs=[vmem_spec()],
        out_specs=vmem_spec(),
        scratch_shapes=[VMEM((members, members), f32), VMEM((members, md), f32)],
        cost_estimate=pl.CostEstimate(
            flops=40_000_000, bytes_accessed=60_000_000, transcendentals=0
        ),
        name="solve",
    )(sums)

    mean_prior = jnp.sum(prior_all, 0, keepdims=True) / members
    anomaly = (prior_all - mean_prior) / spread_root
    change = lax.dot_general(
        gain, anomaly, (((0,), (0,)), ((), ())), precision=exact_mode, preferred_element_type=f32
    )
    posterior = prior_params + change.reshape(md, param_count, block_dev)
    return (posterior, predicted)


def solution(mesh):
    return jax.shard_map(
        shards,
        mesh=mesh,
        in_specs=(
            P("member", None, "basin"),
            P("member", None, "basin"),
            P("basin"),
            P("basin"),
            P("basin"),
            P("basin"),
            P("basin"),
            P(None, "basin"),
            P(None, "basin"),
            P("member", None, "basin"),
        ),
        out_specs=(P("member", None, "basin"), P("member", None, "basin")),
        check_vma=False,
    )
```
